128 devices in a mesh: mem: 32 (over x, z, core), head: 4 (over y).
Axes of the slice: x: 4, y: 4, z: 4, core: 2. Of those that a mesh axis runs over, the one named last changes fastest.
Arguments:
- queries: bfloat16 [512, 32, 128], P('mem', 'head'), may hold values from -170 to 170
- cache_blocks: bfloat16 [1024, 2, 8, 64, 128], P('mem', None, 'head'), may hold values from -9 to 9
- selected: int32 [512, 32], P('mem'), may hold values from 0 to 1023, as said below
- counts: int32 [16, 1024], P(None, 'mem'), may hold values from 0 to 8
- output_weight: bfloat16 [4096, 4096], P('head'), may hold values from -0.09375 to 0.09375
Outputs:
- layer_out: bfloat16 [512, 4096], P('mem', 'head')
- block_heat: float32 [1024], P('mem')
The draws below stay inside these ranges and needn't reach their ends.
Inputs may be any that keep to these rules, and one draw needn't show every extreme that they name: `selected`: each request names 32 different blocks; at most 2 of a request's blocks b share the same b // 32.
All inputs are finite; a program needn't handle non-finite values.
Results may differ from the reference program's by a relative error of at most 0.012.
Values may be sent and summed in bfloat16 or wider, within the bound.
A program may use at most 128 MiB of HBM per device.

```python
import jax
import jax.numpy as jnp
from jax import lax

D = 4096
QUERY_HEADS = 32
KEY_VALUE_HEADS = 8
HEAD_SIZE = 128
BLOCK_TOKENS = 64
SEL = 32
HIST = 16
BLK_DEV = 32
MOST = 2
REQUESTS = 512
TOTAL_KV_BLOCKS = 1024
N_MEM = 32


def pick_blocks(key):
    k_hot, k_pool, k_within, k_order = jax.random.split(key, 4)
    hot_device = jax.random.randint(k_hot, (), 0, N_MEM).astype(jnp.int32)
    others = (hot_device + 1 + jnp.arange(N_MEM - 1, dtype=jnp.int32)) % N_MEM
    candidates = jnp.tile(others, MOST)
    spread = candidates.shape[0]
    shuffled = jax.random.randint(k_pool, (REQUESTS, spread), 0, 1 << 20) * spread + jnp.arange(spread, dtype=jnp.int32)[None, :]
    ordering = jnp.argsort(shuffled, axis=1)
    remaining = candidates[ordering[:, :SEL - MOST]]
    target = jnp.concatenate([jnp.full((REQUESTS, MOST), hot_device, jnp.int32), remaining], axis=1)
    onehot = (target[:, :, None] == jnp.arange(N_MEM, dtype=jnp.int32)[None, None, :]).astype(jnp.int32)
    ranking = jnp.sum((jnp.cumsum(onehot, axis=1) - onehot) * onehot, axis=2)
    inner_keys = jax.random.randint(k_within, (REQUESTS, N_MEM, BLK_DEV), 0, 1 << 20) * BLK_DEV + jnp.arange(BLK_DEV, dtype=jnp.int32)
    within = jnp.argsort(inner_keys, axis=2).astype(jnp.int32)
    chosen = within[jnp.arange(REQUESTS)[:, None], target, ranking]
    block_ids = target * BLK_DEV + chosen
    final_keys = jax.random.randint(k_order, (REQUESTS, SEL), 0, 1 << 20) * SEL + jnp.arange(SEL, dtype=jnp.int32)[None, :]
    return jnp.take_along_axis(block_ids, jnp.argsort(final_keys, axis=1), axis=1).astype(jnp.int32)


def cache_values(key):
    value_vectors = jax.random.truncated_normal(key, -4.5, 4.5, (TOTAL_KV_BLOCKS, 2, KEY_VALUE_HEADS, BLOCK_TOKENS, HEAD_SIZE), jnp.float32)
    return value_vectors


def draw_selected(key, part):
    return pick_blocks(jax.random.fold_in(key, 7))


def draw_cache_blocks(key, part):
    return cache_values(jax.random.fold_in(key, 11)).astype(jnp.bfloat16)


def draw_queries(key, part):
    value_vectors = jax.random.truncated_normal(jax.random.fold_in(key, 3), -4.5, 4.5, (REQUESTS, QUERY_HEADS, HEAD_SIZE), jnp.float32)
    return value_vectors.astype(jnp.bfloat16)


def place_ends(drawn, stream_key, low, high):
    spot = [jax.random.randint(jax.random.fold_in(stream_key, axis), (), 0, length) for axis, length in enumerate(drawn.shape)]
    longest = drawn.shape.index(max(drawn.shape))
    beside = spot[:longest] + [(spot[longest] + 1) % drawn.shape[longest]] + spot[longest + 1:]
    return drawn.at[tuple(spot)].set(low).at[tuple(beside)].set(high)


def block_levels(key, dims, cuts, low, top_value):
    factor_of = 1.0
    for axis_at, shards_of in cuts:
        heights = jax.random.uniform(jax.random.fold_in(jax.random.fold_in(key, 6), axis_at), (shards_of,), jnp.float32, low / len(cuts), top_value / len(cuts))
        factor_of = factor_of * jnp.repeat(jnp.exp(heights), dims[axis_at] // shards_of).reshape((-1,) + (1,) * (len(dims) - 1 - axis_at))
    return factor_of


def noise(rng, dims, scale, reach, cuts=(), held_as=jnp.bfloat16):
    values = jax.random.normal(rng, dims, jnp.float32) * scale
    if len(cuts) > 0:
        values = block_levels(rng, dims, cuts, -0.22, 0.18) * values
    return jnp.clip(values, min=-reach, max=reach).astype(held_as)


def setup_inputs(seed: int = 0) -> dict:
    key_list = jax.random.split(jax.random.key(seed), 6)
    return {
        "queries": draw_queries(jax.random.fold_in(key_list[5], 71), 0),
        "cache_blocks": draw_cache_blocks(jax.random.fold_in(key_list[5], 71), 0),
        "selected": draw_selected(jax.random.fold_in(key_list[5], 71), 0),
        "counts": place_ends(jax.random.randint(key_list[3], (HIST, TOTAL_KV_BLOCKS), 0, 9), jax.random.fold_in(key_list[3], 1), 0, 8).astype(jnp.int32),
        "output_weight": noise(key_list[4], (QUERY_HEADS * HEAD_SIZE, D), (QUERY_HEADS * HEAD_SIZE) ** -0.5, 0.09375, ((0, 4),)),
    }


def block_partial(single_query_row, key_rows, value_rows):
    group_stacked = single_query_row.astype(jnp.float32).reshape(KEY_VALUE_HEADS, QUERY_HEADS // KEY_VALUE_HEADS, HEAD_SIZE)
    scores = jnp.einsum("hgd,htd->hgt", group_stacked, key_rows.astype(jnp.float32)) * (HEAD_SIZE ** -0.5)
    peak_score = jnp.max(scores, axis=-1)
    expo_terms = jnp.exp(scores - peak_score[..., None])
    totals = jnp.sum(expo_terms, axis=-1)
    weights = lax.optimization_barrier(expo_terms.astype(jnp.bfloat16)).astype(jnp.float32)
    outputs = jnp.einsum("hgt,htd->hgd", weights, value_rows.astype(jnp.float32))
    return peak_score, totals, outputs


def reference(queries, cache_blocks, selected, counts, output_weight):
    def one_request(inputs):
        single_query_row, chosen = inputs
        blocks = cache_blocks[chosen]
        peak_score, totals, outputs = jax.vmap(block_partial, in_axes=(None, 0, 0))(single_query_row, blocks[:, 0], blocks[:, 1])
        highest = jnp.max(peak_score, axis=0)
        factor = jnp.exp(peak_score - highest)
        denominator = jnp.sum(factor * totals, axis=0)
        numerator = jnp.sum(factor[..., None] * outputs, axis=0)
        return (numerator / denominator[..., None]).reshape(QUERY_HEADS * HEAD_SIZE).astype(jnp.bfloat16)

    attended = lax.map(one_request, (queries, selected))
    layer_out = jnp.dot(attended, output_weight, preferred_element_type=jnp.float32).astype(jnp.bfloat16)
    access_hits = jnp.zeros((TOTAL_KV_BLOCKS,), jnp.float32).at[selected.reshape(-1)].add(1.0)
    decays = 0.5 ** jnp.arange(HIST, dtype=jnp.float32)
    block_heat = jnp.sum(decays[:, None] * counts.astype(jnp.float32), axis=0) + access_hits
    return layer_out, block_heat
```

```python
import functools
import math

import jax
import jax.numpy as jnp
from jax import lax
from jax.experimental import pallas as pl
from jax.experimental.pallas import tpu as pltpu
from jax.sharding import PartitionSpec as P

MESH = pl.DeviceIdType.MESH
NEG = -1e30
LOG2E = 1.4426950408889634


def ring_order(i):
    return i + (i // 2) * (1 - 2 * (i % 2))


def kernel(
    side, heads_n, scale,
    q_hbm, kv_hbm, sel_hbm, cnt_hbm, w_hbm,
    out_ref, heat_ref,
    qin, qout, sin, sout, kv, cnt, w,
    meta_v, meta_s, own, own_ml, part, part_ml, sib, sib_ml, comb, comb_ml, ret, ret_ml,
    att, ysend, yrecv,
    lsem, msem,
    in_s, in_r, fw_s, fw_r, sb_s, sb_r, rt_s, rt_r, y_s, y_r,
):
    n = side * side
    reqs, heads = q_hbm.shape[0], q_hbm.shape[1]
    dim = q_hbm.shape[2]
    blocks = kv.shape[0]
    tok = kv.shape[2]
    group = heads // 2
    me = lax.axis_index("mem")
    y = lax.axis_index("head")
    core = me % 2
    chip = me // 2
    cx, cz = chip // side, chip % side
    sibling = me + 1 - 2 * core

    def at(k, sign):
        dx, dz = k // side, k % side
        if side == 4:
            dx, dz = ring_order(dx), ring_order(dz)
        px = (cx + sign * dx + side) % side
        pz = (cz + sign * dz + side) % side
        return (px * side + pz) * 2 + core

    def remote(src, dst, ss, rs, **device):
        return pltpu.make_async_remote_copy(
            src_ref=src, dst_ref=dst, send_sem=ss, recv_sem=rs,
            device_id=device, device_id_type=MESH,
        )

    loc = [
        pltpu.make_async_copy(sel_hbm, sin.at[0], lsem.at[0]),
        pltpu.make_async_copy(q_hbm, qin.at[0], lsem.at[1]),
        pltpu.make_async_copy(kv_hbm, kv, lsem.at[2]),
        pltpu.make_async_copy(cnt_hbm, cnt, lsem.at[3]),
    ]
    for c in loc:
        c.start()

    barrier = pltpu.get_barrier_semaphore()
    pl.semaphore_signal(barrier, inc=1, device_id={"mem": sibling}, device_id_type=MESH)

    @pl.loop(1, n)
    def _(k):
        pl.semaphore_signal(barrier, inc=1, device_id={"mem": at(k, 1)}, device_id_type=MESH)

    for j in range(1, heads_n):
        pl.semaphore_signal(
            barrier, inc=1, device_id={"head": (y + j) % heads_n}, device_id_type=MESH
        )
    pl.semaphore_wait(barrier, n + heads_n - 1)

    def fw(k, stream, from_hbm=False):
        src, dst = ((sin, sout), (qin, qout))[stream]
        src = (sel_hbm, q_hbm)[stream] if from_hbm else src.at[k]
        return remote(src, dst.at[k], fw_s.at[stream, k], fw_r.at[stream, k], mem=sibling)

    def plane(k, stream):
        src, dst = ((sel_hbm, sin), (q_hbm, qin))[stream]
        return remote(src, dst.at[k], in_s.at[stream, k], in_r.at[stream, k], mem=at(k, 1))

    for s in range(2):
        fw(0, s, True).start()

    @pl.loop(1, n)
    def _(k):
        for s in range(2):
            plane(k, s).start()

    wcopies = [
        pltpu.make_async_copy(
            w_hbm.at[:, pl.ds(pl.multiple_of(((y + j) % heads_n) * out_ref.shape[1], 128), out_ref.shape[1])],
            w.at[j], lsem.at[4 + j],
        )
        for j in range(heads_n)
    ]
    for c in wcopies:
        c.start()

    row = lax.broadcasted_iota(jnp.int32, (heads, 2 * tok // 2), 0)
    lane = lax.broadcasted_iota(jnp.int32, (heads, 2 * tok // 2), 1)
    kmask = (row // group) == (lane // (tok // 2))
    lane_r = lax.broadcasted_iota(jnp.int32, (reqs, 128), 1)
    row_r = lax.broadcasted_iota(jnp.int32, (reqs, 128), 0)
    lane_h = lax.broadcasted_iota(jnp.int32, (heads, 128), 1)
    c2 = scale * LOG2E

    def table(sel_ref, slot, k, hits):
        sel = sel_ref[k]
        here = (sel // blocks) == me
        local = sel % blocks
        first = jnp.min(jnp.where(here, local, blocks), axis=1, keepdims=True)
        last = jnp.max(jnp.where(here, local, -1), axis=1, keepdims=True)
        b0 = jnp.broadcast_to(jnp.where(first < blocks, first, -1), (reqs, 128))
        b1 = jnp.broadcast_to(jnp.where(last > first, last, -1), (reqs, 128))
        hits = hits + (b0 == lane_r).astype(jnp.float32) + (b1 == lane_r).astype(jnp.float32)
        line = jnp.where(lane_r == row_r, b0, 0) + jnp.where(lane_r == row_r + reqs, b1, 0)
        meta_v[slot, k] = jnp.sum(line, axis=0, keepdims=True)
        pltpu.make_async_copy(meta_v.at[slot, k], meta_s.at[slot, k], msem.at[slot, k]).start()
        return hits

    def attend(q_ref, slot, k, emit):
        pltpu.make_async_copy(meta_v.at[slot, k], meta_s.at[slot, k], msem.at[slot, k]).wait()
        ml = jnp.zeros((heads, 128), jnp.float32)
        for r in range(reqs):
            b0 = meta_s[slot, k, 0, r]
            b1 = meta_s[slot, k, 0, reqs + r]
            i0, i1 = jnp.maximum(b0, 0), jnp.maximum(b1, 0)
            off0 = jnp.where(b0 < 0, NEG, 0.0)
            off1 = jnp.where(b1 < 0, NEG, 0.0)
            q = q_ref[k, r]
            dims = (((1,), (1,)), ((), ()))
            s0 = lax.dot_general(q, kv[i0, 0], dims, preferred_element_type=jnp.float32)
            s1 = lax.dot_general(q, kv[i1, 0], dims, preferred_element_type=jnp.float32)
            s0 = jnp.where(kmask, s0 + off0, NEG)
            s1 = jnp.where(kmask, s1 + off1, NEG)
            m = jnp.max(jnp.maximum(s0, s1), axis=1, keepdims=True)
            p0 = jnp.exp2((s0 - m) * c2)
            p1 = jnp.exp2((s1 - m) * c2)
            l = jnp.sum(p0 + p1, axis=1, keepdims=True)
            o = jnp.dot(p0.astype(jnp.bfloat16), kv[i0, 1], preferred_element_type=jnp.float32)
            o += jnp.dot(p1.astype(jnp.bfloat16), kv[i1, 1], preferred_element_type=jnp.float32)
            emit(r, o)
            ml = jnp.where(lane_h == r, m, ml)
            ml = jnp.where(lane_h == reqs + r, l, ml)
        return ml

    def to_sibling(k):
        return (
            remote(part.at[k], sib.at[k], sb_s.at[0, k], sb_r.at[0, k], mem=sibling),
            remote(part_ml.at[k], sib_ml.at[k], sb_s.at[1, k], sb_r.at[1, k], mem=sibling),
        )

    def to_owner(k):
        return (
            remote(comb.at[k], ret.at[k], rt_s.at[0, k], rt_r.at[0, k], mem=at(k, -1)),
            remote(comb_ml.at[k], ret_ml.at[k], rt_s.at[1, k], rt_r.at[1, k], mem=at(k, -1)),
        )

    loc[0].wait()
    loc[1].wait()
    loc[2].wait()

    def step(t, hits):
        def arrive_in(hits):
            @pl.when(t > 0)
            def _():
                for s in range(2):
                    plane(t, s).wait_recv()
                    fw(t, s).start()
            return table(sin, 0, t, hits)

        hits = lax.cond(t < n, arrive_in, lambda h: h, hits)

        def arrive_out(hits):
            for s in range(2):
                fw(t - 1, s).wait_recv()
            return table(sout, 1, t - 1, hits)

        hits = lax.cond((t >= 1) & (t - 1 < n), arrive_out, lambda h: h, hits)

        @pl.when((t >= 2) & (t - 2 < n))
        def _():
            k = t - 2

            def emit_part(r, o):
                part[k, r] = o.astype(jnp.bfloat16)

            part_ml[k] = attend(qout, 1, k, emit_part)

            def emit_own(r, o):
                own[k, r] = o

            own_ml[k] = attend(qin, 0, k, emit_own)
            for c in to_sibling(k):
                c.start()

        @pl.when(t >= 4)
        def _():
            k = t - 4
            for c in to_sibling(k):
                c.wait_recv()
            a, b = own_ml[k], sib_ml[k]
            top = jnp.maximum(a, b)
            fa, fb = jnp.exp2((a - top) * c2), jnp.exp2((b - top) * c2)
            total = pltpu.roll(fa, reqs, 1) * a + pltpu.roll(fb, reqs, 1) * b
            comb_ml[k] = jnp.where(lane_h < reqs, top, total)
            for r in range(reqs):
                o = own[k, r] * fa[:, r : r + 1] + sib[k, r].astype(jnp.float32) * fb[:, r : r + 1]
                comb[k, r] = o.astype(jnp.bfloat16)

            @pl.when(k > 0)
            def _():
                for c in to_owner(k):
                    c.start()

        return hits

    hits = lax.fori_loop(0, n + 4, step, jnp.zeros((reqs, 128), jnp.float32))

    loc[3].wait()
    counts = cnt[...].astype(jnp.float32)
    decay = jnp.exp2(-lax.broadcasted_iota(jnp.int32, counts.shape, 0).astype(jnp.float32))
    heat_ref[...] = (
        jnp.sum(decay * counts, axis=0, keepdims=True)
        + jnp.sum(hits, axis=0, keepdims=True)[:, : counts.shape[1]]
    )

    ret[0] = comb[0]
    ret_ml[0] = comb_ml[0]

    @pl.loop(1, n)
    def _(k):
        for c in to_owner(k):
            c.wait_recv()

    top = ret_ml[0]
    for k in range(1, n):
        top = jnp.maximum(top, ret_ml[k])
    den = jnp.zeros((heads, 128), jnp.float32)
    for k in range(n):
        f = jnp.exp2((ret_ml[k] - top) * c2)
        den += f * pltpu.roll(ret_ml[k], 128 - reqs, 1)
    inv = 1.0 / den
    for r in range(reqs):
        att[r] = jnp.zeros((heads, dim), jnp.float32)

    @pl.loop(0, n)
    def _(k):
        f = jnp.exp2((ret_ml[k] - top) * c2) * inv
        for r in range(reqs):
            att[r] += ret[k, r].astype(jnp.float32) * f[:, r : r + 1]

    lhs = jnp.concatenate(
        [att[:, h, :].astype(jnp.bfloat16) for h in range(heads)], axis=1
    )

    for c in wcopies:
        c.wait()

    def y_copy(j):
        return remote(ysend.at[j], yrecv.at[j], y_s.at[j], y_r.at[j], head=(y + j) % heads_n)

    for j in range(1, heads_n):
        ysend[j] = jnp.dot(lhs, w[j], preferred_element_type=jnp.float32).astype(jnp.bfloat16)
        y_copy(j).start()
    total = jnp.dot(lhs, w[0], preferred_element_type=jnp.float32).astype(jnp.bfloat16).astype(jnp.float32)
    for j in range(1, heads_n):
        y_copy(j).wait()
        total += yrecv[j].astype(jnp.float32)
    out_ref[...] = total.astype(out_ref.dtype)

    for s in range(2):
        fw(0, s, True).wait_send()

    @pl.loop(0, n)
    def _(k):
        for c in to_sibling(k):
            c.wait_send()

        @pl.when(k > 0)
        def _():
            for s in range(2):
                fw(k, s).wait_send()
                plane(k, s).wait_send()
            for c in to_owner(k):
                c.wait_send()


def per_device(side, heads_n, queries, cache_blocks, selected, counts, output_weight):
    reqs, heads, dim = queries.shape
    blocks = cache_blocks.shape[0]
    tok = cache_blocks.shape[2] * cache_blocks.shape[3]
    kv = cache_blocks.reshape(blocks, 2, tok, dim)
    n = side * side
    cols = output_weight.shape[1] // heads_n
    bf, f32, i32 = jnp.bfloat16, jnp.float32, jnp.int32
    any_ = pl.BlockSpec(memory_space=pl.ANY)
    vmem = pl.BlockSpec(memory_space=pltpu.VMEM)
    dma = pltpu.SemaphoreType.DMA
    out, heat = pl.pallas_call(
        functools.partial(kernel, side, heads_n, dim ** -0.5),
        out_shape=(
            jax.ShapeDtypeStruct((reqs, cols), bf),
            jax.ShapeDtypeStruct((1, blocks), f32),
        ),
        in_specs=[any_] * 5,
        out_specs=(vmem, vmem),
        scratch_shapes=[
            pltpu.VMEM((n, reqs, heads, dim), bf),
            pltpu.VMEM((n, reqs, heads, dim), bf),
            pltpu.VMEM((n,) + selected.shape, i32),
            pltpu.VMEM((n,) + selected.shape, i32),
            pltpu.VMEM(kv.shape, bf),
            pltpu.VMEM(counts.shape, i32),
            pltpu.VMEM((heads_n, output_weight.shape[0], cols), bf),
            pltpu.VMEM((2, n, 1, 128), i32),
            pltpu.SMEM((2, n, 1, 128), i32),
            pltpu.VMEM((n, reqs, heads, dim), f32),
            pltpu.VMEM((n, heads, 128), f32),
            pltpu.VMEM((n, reqs, heads, dim), bf),
            pltpu.VMEM((n, heads, 128), f32),
            pltpu.VMEM((n, reqs, heads, dim), bf),
            pltpu.VMEM((n, heads, 128), f32),
            pltpu.VMEM((n, reqs, heads, dim), bf),
            pltpu.VMEM((n, heads, 128), f32),
            pltpu.VMEM((n, reqs, heads, dim), bf),
            pltpu.VMEM((n, heads, 128), f32),
            pltpu.VMEM((reqs, heads, dim), f32),
            pltpu.VMEM((heads_n, reqs, cols), bf),
            pltpu.VMEM((heads_n, reqs, cols), bf),
            dma((4 + heads_n,)), dma((2, n)),
            dma((2, n)), dma((2, n)), dma((2, n)), dma((2, n)),
            dma((2, n)), dma((2, n)), dma((2, n)), dma((2, n)),
            dma((heads_n,)), dma((heads_n,)),
        ],
        compiler_params=pltpu.CompilerParams(collective_id=0, has_side_effects=True),
    )(queries, kv, selected, counts, output_weight)
    return out, heat.reshape(blocks)


def solution(mesh):
    side = math.isqrt(mesh.shape["mem"] // 2)
    return jax.shard_map(
        functools.partial(per_device, side, mesh.shape["head"]),
        mesh=mesh,
        in_specs=(
            P("mem", "head", None),
            P("mem", None, "head", None, None),
            P("mem", None),
            P(None, "mem"),
            P("head", None),
        ),
        out_specs=(P("mem", "head"), P("mem")),
        check_vma=False,
    )
```

```python
import functools
import math

import jax
import jax.numpy as jnp
from jax import lax
from jax.experimental import pallas as pl
from jax.experimental.pallas import tpu as pltpu
from jax.sharding import PartitionSpec as P

MESH = pl.DeviceIdType.MESH
NEG = -1e30
LOG2E = 1.4426950408889634


def offsets_in_order(side):
    far = list(range(2, side - 1))
    near = [1] + ([side - 1] if side > 2 else [])
    row = near + far
    order = [(0, 0)] + [(dx, 0) for dx in row]
    for dz in far:
        order += [(dx, dz) for dx in [0] + row]
    order += [(dx, dz) for dx in row for dz in near]
    return order + [(0, dz) for dz in near]


def kernel(
    side, heads_n, scale, later,
    q_hbm, kv_hbm, sel_hbm, cnt_hbm, w_hbm,
    out_ref, heat_ref,
    qin, qout, tin, tout, town, sel_v, kv, kt, cnt, w, hits,
    meta_s, p_in, p_out, own, own_ml, part, part_ml, sib, sib_ml, comb, comb_ml, ret, ret_ml,
    att, ysend, yrecv,
    lsem, msem,
    in_s, in_r, fw_s, fw_r, sb_s, sb_r, rt_s, rt_r, y_s, y_r,
):
    bf, f32, i32 = jnp.bfloat16, jnp.float32, jnp.int32
    n = side * side
    order = offsets_in_order(side)
    reqs, heads, dim = q_hbm.shape
    blocks, tok = kv.shape[0], kv.shape[2]
    group = heads // 2
    cols = out_ref.shape[1]
    me = lax.axis_index("mem")
    y = lax.axis_index("head")
    core = me % 2
    chip = me // 2
    cx, cz = chip // side, chip % side
    sibling = me + 1 - 2 * core
    line = cz * 2 + core
    c2 = scale * LOG2E

    def chip_at(dx, dz):
        px = (cx + dx + side) % side
        pz = (cz + dz + side) % side
        return (px * side + pz) * 2 + core

    def pick(values, k):
        if isinstance(k, int):
            return values[k]
        found = i32(values[0])
        for i in range(1, n):
            found = jnp.where(k == i, i32(values[i]), found)
        return found

    def remote(src, dst, ss, rs, **device):
        return pltpu.make_async_remote_copy(
            src_ref=src, dst_ref=dst, send_sem=ss, recv_sem=rs,
            device_id=device, device_id_type=MESH,
        )

    def fw(k, stream, first=False):
        src, dst = ((tin, tout), (qin, qout))[stream]
        src = (town.at[cx], q_hbm)[stream] if first else src.at[k]
        return remote(src, dst.at[k], fw_s.at[stream, k], fw_r.at[stream, k], mem=sibling)

    def plane(k, stream):
        dx, dz = order[k]
        dst = (tin, qin)[stream]
        if dz == 0:
            src = (town.at[(cx + dx) % side], q_hbm)[stream]
            peer = chip_at(dx, 0)
        elif dx == 0:
            src = (town.at[cx], q_hbm)[stream]
            peer = chip_at(0, dz)
        else:
            src = dst.at[order.index((dx, 0))]
            peer = chip_at(0, dz)
        return remote(src, dst.at[k], in_s.at[stream, k], in_r.at[stream, k], mem=peer)

    def arrived(k, stream):
        dst = (tin, qin)[stream]
        return remote(dst.at[k], dst.at[k], in_s.at[stream, k], in_r.at[stream, k], mem=sibling)

    def meta(k, slot):
        src = (tin, tout)[slot]
        return pltpu.make_async_copy(
            src.at[k, pl.ds(line, 1)], meta_s.at[slot, k], msem.at[slot, k]
        )

    def to_sibling(k):
        return (
            remote(part.at[k], sib.at[k], sb_s.at[0, k], sb_r.at[0, k], mem=sibling),
            remote(part_ml.at[k], sib_ml.at[k], sb_s.at[1, k], sb_r.at[1, k], mem=sibling),
        )

    def to_owner(k):
        peer = chip_at(-pick([d[0] for d in order], k), -pick([d[1] for d in order], k))
        return (
            remote(comb.at[k], ret.at[k], rt_s.at[0, k], rt_r.at[0, k], mem=peer),
            remote(comb_ml.at[k], ret_ml.at[k], rt_s.at[1, k], rt_r.at[1, k], mem=peer),
        )

    loc = [
        pltpu.make_async_copy(sel_hbm, sel_v, lsem.at[0]),
        pltpu.make_async_copy(kv_hbm, kv, lsem.at[1]),
        pltpu.make_async_copy(q_hbm, qin.at[0], lsem.at[2]),
        pltpu.make_async_copy(cnt_hbm, cnt, lsem.at[3]),
    ]
    for c in loc:
        c.start()

    barrier = pltpu.get_barrier_semaphore()
    pl.semaphore_signal(barrier, inc=1, device_id={"mem": sibling}, device_id_type=MESH)
    for d in range(1, side):
        for peer in (chip_at(d, 0), chip_at(0, d)):
            pl.semaphore_signal(barrier, inc=1, device_id={"mem": peer}, device_id_type=MESH)
    for j in range(1, heads_n):
        pl.semaphore_signal(
            barrier, inc=1, device_id={"head": (y + j) % heads_n}, device_id_type=MESH
        )

    devices = 2 * n
    loc[0].wait()
    sel = sel_v[...]
    target, local = sel // blocks, sel % blocks
    dev = lax.broadcasted_iota(i32, (devices, sel.shape[1]), 0)
    lane_d = lax.broadcasted_iota(i32, (devices, 128), 1)
    table = jnp.full((devices, 128), -1, i32)
    for r in range(reqs):
        here = target[r : r + 1] == dev
        value = jnp.broadcast_to(local[r : r + 1], dev.shape)
        first = jnp.min(jnp.where(here, value, blocks), axis=1, keepdims=True)
        last = jnp.max(jnp.where(here, value, -1), axis=1, keepdims=True)
        table = jnp.where((lane_d == r) & (first < blocks), first, table)
        table = jnp.where((lane_d == reqs + r) & (last > first), last, table)
    for d in range(side):
        town[d] = table[d * 2 * side : (d + 1) * 2 * side]
    tin[0] = town[cx]
    meta(0, 0).start()

    pl.semaphore_wait(barrier, 2 * (side - 1) + heads_n)

    for k in list(range(1, side)) + [i for i in range(n) if i and order[i][0] == 0]:
        for s in range(2):
            plane(k, s).start()
    for s in range(2):
        fw(0, s, True).start()

    wcopies = [
        pltpu.make_async_copy(
            w_hbm.at[:, pl.ds(pl.multiple_of(((y + j) % heads_n) * cols, 128), cols)],
            w.at[j], lsem.at[4 + j],
        )
        for j in range(heads_n)
    ]
    for c in wcopies:
        c.start()

    row = lax.broadcasted_iota(i32, (heads, tok), 0)
    lane = lax.broadcasted_iota(i32, (heads, tok), 1)
    kmask = (row // group) == (lane // (tok // 2))
    lane_h = lax.broadcasted_iota(i32, (heads, 128), 1)
    brow = lax.broadcasted_iota(i32, (blocks, 128), 0)
    zero = jnp.zeros((heads, dim), bf)

    def four(a, b, c, d):
        return jnp.concatenate(
            [jnp.concatenate([a, b], axis=1), jnp.concatenate([c, d], axis=1)], axis=0
        )

    def softmax(s0, s1, off0, off1):
        s0 = jnp.where(kmask, s0 + off0, NEG)
        s1 = jnp.where(kmask, s1 + off1, NEG)
        m = jnp.max(jnp.maximum(s0, s1), axis=1, keepdims=True)
        p0, p1 = jnp.exp2((s0 - m) * c2), jnp.exp2((s1 - m) * c2)
        return p0, p1, m, jnp.sum(p0 + p1, axis=1, keepdims=True)

    def scores(q_ref, slot, k, p_ref, ml_ref):
        ml = jnp.zeros((heads, 128), f32)
        for r in range(0, reqs, 2):
            ids = [meta_s[slot, k, 0, i] for i in (r, reqs + r, r + 1, reqs + r + 1)]
            off = [jnp.where(b < 0, NEG, 0.0) for b in ids]
            k0, k1, k2, k3 = [kt[jnp.maximum(b, 0)] for b in ids]
            lhs = four(q_ref[k, r], zero, zero, q_ref[k, r + 1])
            s = jnp.dot(lhs, four(k0, k1, k2, k3), preferred_element_type=f32)
            a0, a1, ma, la = softmax(s[:heads, :tok], s[:heads, tok:], off[0], off[1])
            b0, b1, mb, lb = softmax(s[heads:, :tok], s[heads:, tok:], off[2], off[3])
            p_ref[r // 2] = jnp.concatenate(
                [jnp.concatenate([a0, b0], axis=0).astype(bf), jnp.concatenate([a1, b1], axis=0).astype(bf)],
                axis=1,
            )
            for i, v in ((r, ma), (reqs + r, la), (r + 1, mb), (reqs + r + 1, lb)):
                ml = jnp.where(lane_h == i, v, ml)
        ml_ref[k] = ml

    def values(slot, k, p_list, emit):
        for r in range(0, reqs, 2):
            ids = [meta_s[slot, k, 0, i] for i in (r, reqs + r, r + 1, reqs + r + 1)]
            v0, v1, v2, v3 = [kv[jnp.maximum(b, 0), 1] for b in ids]
            o = jnp.dot(p_list[r // 2], four(v0, v2, v1, v3), preferred_element_type=f32)
            emit(k, r, o[:heads, :dim])
            emit(k, r + 1, o[heads:, dim:])

    def emit_own(k, r, o):
        own[k, r] = o

    def emit_part(k, r, o):
        part[k, r] = o.astype(bf)

    def load(p_ref):
        return [p_ref[i] for i in range(reqs // 2)]

    def count(k):
        for t in (tin, tout):
            hits[...] += jnp.where(t[k, pl.ds(line, 1)] == brow, 1.0, 0.0)

    def combine(k):
        a, b = own_ml[k], sib_ml[k]
        top = jnp.maximum(a, b)
        fa, fb = jnp.exp2((a - top) * c2), jnp.exp2((b - top) * c2)
        total = pltpu.roll(fa, reqs, 1) * a + pltpu.roll(fb, reqs, 1) * b
        comb_ml[k] = jnp.where(lane_h < reqs, top, total)
        for r in range(reqs):
            o = own[k, r] * fa[:, r : r + 1] + sib[k, r].astype(f32) * fb[:, r : r + 1]
            comb[k, r] = o.astype(bf)

    def send_owner(k):
        for c in to_owner(k):
            c.start()

    loc[1].wait()

    @pl.loop(0, blocks // 4)
    def _(b):
        for i in range(4):
            kt[b * 4 + i] = kv[b * 4 + i, 0].T

    hits[...] = jnp.zeros(hits.shape, f32)
    loc[2].wait()
    meta(0, 0).wait()
    scores(qin, 0, 0, p_in, own_ml)

    for k in range(1, side):
        for s in range(2):
            arrived(k, s).wait_recv()
            for i in range(n):
                if order[i][0] == order[k][0] and order[i][1]:
                    plane(i, s).start()
            fw(k, s).start()
        meta(k, 0).start()

    for s in range(2):
        fw(0, s).wait_recv()
    meta(0, 1).start()
    meta(0, 1).wait()
    scores(qout, 1, 0, p_out, part_ml)
    values(1, 0, load(p_out), emit_part)
    for c in to_sibling(0):
        c.start()
    count(0)
    fw(1, 0).wait_recv()
    meta(1, 1).start()

    @pl.loop(1, n)
    def _(t):
        ahead = t + side - 1

        @pl.when(ahead < n)
        def _():
            for s in range(2):
                arrived(ahead, s).wait_recv()
                fw(ahead, s).start()
            meta(ahead, 0).start()

        @pl.when(t + 1 < n)
        def _():
            fw(t + 1, 0).wait_recv()
            meta(t + 1, 1).start()

        @pl.when(t >= 2)
        def _():
            for c in to_sibling(t - 2):
                c.wait_recv()

        fw(t, 1).wait_recv()
        meta(t, 0).wait()
        meta(t, 1).wait()

        p = load(p_in)
        scores(qout, 1, t, p_out, part_ml)
        values(0, t - 1, p, emit_own)
        p = load(p_out)
        scores(qin, 0, t, p_in, own_ml)
        values(1, t, p, emit_part)
        count(t)
        for c in to_sibling(t):
            c.start()

        @pl.when(t >= 2)
        def _():
            combine(t - 2)

        @pl.when(t >= 3)
        def _():
            send_owner(t - 2)

    values(0, n - 1, load(p_in), emit_own)
    for k in (n - 2, n - 1):
        for c in to_sibling(k):
            c.wait_recv()
        combine(k)
        send_owner(k)

    loc[3].wait()
    counts = cnt[...].astype(f32)
    decay = jnp.exp2(-lax.broadcasted_iota(i32, counts.shape, 0).astype(f32))
    here = jnp.broadcast_to(jnp.sum(hits[...], axis=1, keepdims=True), (blocks, blocks))
    eye = lax.broadcasted_iota(i32, (blocks, blocks), 0) == lax.broadcasted_iota(i32, (blocks, blocks), 1)
    heat_ref[...] = jnp.sum(decay * counts, axis=0, keepdims=True) + jnp.sum(
        jnp.where(eye, here, 0.0), axis=0, keepdims=True
    )

    ret[0] = comb[0]
    ret_ml[0] = comb_ml[0]

    def merged(start, stop):
        @pl.loop(max(start, 1), stop)
        def _(k):
            for c in to_owner(k):
                c.wait_recv()

        top = ret_ml[start]
        for k in range(start + 1, stop):
            top = jnp.maximum(top, ret_ml[k])
        den = jnp.zeros((heads, 128), f32)
        acc = [jnp.zeros((heads, dim), f32)] * reqs

        def add(k, carry):
            den, acc = carry
            f = jnp.exp2((ret_ml[k] - top) * c2)
            den += f * pltpu.roll(ret_ml[k], 128 - reqs, 1)
            return den, [acc[r] + ret[k, r].astype(f32) * f[:, r : r + 1] for r in range(reqs)]

        den, acc = lax.fori_loop(start, stop, add, (den, acc))
        return top, den, acc

    top_a, den_a, acc_a = merged(0, n - later)
    top_b, den_b, acc_b = merged(n - later, n)
    top = jnp.maximum(top_a, top_b)
    fa, fb = jnp.exp2((top_a - top) * c2), jnp.exp2((top_b - top) * c2)
    inv = 1.0 / (fa * den_a + fb * den_b)
    fa, fb = fa * inv, fb * inv
    for r in range(reqs):
        att[r] = acc_a[r] * fa[:, r : r + 1] + acc_b[r] * fb[:, r : r + 1]

    lhs = jnp.concatenate([att[:, h, :].astype(bf) for h in range(heads)], axis=1)

    for c in wcopies:
        c.wait()

    def y_copy(j):
        return remote(ysend.at[j], yrecv.at[j], y_s.at[j], y_r.at[j], head=(y + j) % heads_n)

    for j in range(1, heads_n):
        ysend[j] = jnp.dot(lhs, w[j], preferred_element_type=f32).astype(bf)
        y_copy(j).start()
    total = jnp.dot(lhs, w[0], preferred_element_type=f32).astype(bf).astype(f32)
    for j in range(1, heads_n):
        y_copy(j).wait()
        total += yrecv[j].astype(f32)
    out_ref[...] = total.astype(out_ref.dtype)

    for s in range(2):
        fw(0, s, True).wait_send()
        for k in range(1, n):
            plane(k, s).wait_send()

    @pl.loop(0, n)
    def _(k):
        for c in to_sibling(k):
            c.wait_send()

        @pl.when(k > 0)
        def _():
            for s in range(2):
                fw(k, s).wait_send()
            for c in to_owner(k):
                c.wait_send()


def per_device(side, heads_n, queries, cache_blocks, selected, counts, output_weight):
    reqs, heads, dim = queries.shape
    blocks = cache_blocks.shape[0]
    tok = cache_blocks.shape[2] * cache_blocks.shape[3]
    kv = cache_blocks.reshape(blocks, 2, tok, dim)
    n = side * side
    cols = output_weight.shape[1] // heads_n
    bf, f32, i32 = jnp.bfloat16, jnp.float32, jnp.int32
    any_ = pl.BlockSpec(memory_space=pl.ANY)
    vmem = pl.BlockSpec(memory_space=pltpu.VMEM)
    dma = pltpu.SemaphoreType.DMA
    rows = pltpu.VMEM((n, reqs, heads, dim), bf)
    small = pltpu.VMEM((n, heads, 128), f32)
    tiles = pltpu.VMEM((n, 2 * side, 128), i32)
    out, heat = pl.pallas_call(
        functools.partial(kernel, side, heads_n, dim ** -0.5, max(2, n // 4)),
        out_shape=(
            jax.ShapeDtypeStruct((reqs, cols), bf),
            jax.ShapeDtypeStruct((1, blocks), f32),
        ),
        in_specs=[any_] * 5,
        out_specs=(vmem, vmem),
        scratch_shapes=[
            rows, rows, tiles, tiles,
            pltpu.VMEM((side, 2 * side, 128), i32),
            pltpu.VMEM(selected.shape, i32),
            pltpu.VMEM(kv.shape, bf),
            pltpu.VMEM((blocks, dim, tok), bf),
            pltpu.VMEM(counts.shape, i32),
            pltpu.VMEM((heads_n, output_weight.shape[0], cols), bf),
            pltpu.VMEM((blocks, 128), f32),
            pltpu.SMEM((2, n, 1, 128), i32),
            pltpu.VMEM((reqs // 2, 2 * heads, 2 * tok), bf),
            pltpu.VMEM((reqs // 2, 2 * heads, 2 * tok), bf),
            pltpu.VMEM((n, reqs, heads, dim), f32),
            small, rows, small, rows, small, rows, small, rows, small,
            pltpu.VMEM((reqs, heads, dim), f32),
            pltpu.VMEM((heads_n, reqs, cols), bf),
            pltpu.VMEM((heads_n, reqs, cols), bf),
            dma((4 + heads_n,)), dma((2, n)),
            dma((2, n)), dma((2, n)), dma((2, n)), dma((2, n)),
            dma((2, n)), dma((2, n)), dma((2, n)), dma((2, n)),
            dma((heads_n,)), dma((heads_n,)),
        ],
        compiler_params=pltpu.CompilerParams(collective_id=0, has_side_effects=True),
    )(queries, kv, selected, counts, output_weight)
    return out, heat.reshape(blocks)


def solution(mesh):
    side = math.isqrt(mesh.shape["mem"] // 2)
    return jax.shard_map(
        functools.partial(per_device, side, mesh.shape["head"]),
        mesh=mesh,
        in_specs=(
            P("mem", "head", None),
            P("mem", None, "head", None, None),
            P("mem", None),
            P(None, "mem"),
            P("head", None),
        ),
        out_specs=(P("mem", "head"), P("mem")),
        check_vma=False,
    )
```

```python
import functools
import math

import jax
import jax.numpy as jnp
from jax import lax
from jax.experimental import pallas as pl
from jax.experimental.pallas import tpu as pltpu
from jax.sharding import PartitionSpec as P

MESH = pl.DeviceIdType.MESH
NEG = -1e30
LOG2E = 1.4426950408889634


def offsets_in_order(side):
    far = list(range(2, side - 1))
    near = [1] + ([side - 1] if side > 2 else [])
    order = [(0, 0)] + [(dx, 0) for dx in near + far] + [(0, dz) for dz in far]
    order += [(dx, dz) for dx in near for dz in near]
    order += [(dx, dz) for dx in near for dz in far]
    order += [(dx, dz) for dx in far for dz in near + far]
    return order + [(0, dz) for dz in near]


def kernel(
    side, heads_n, scale, later,
    q_hbm, kv_hbm, sel_hbm, cnt_hbm, w_hbm,
    out_ref, heat_ref,
    qin, qout, tin, tout, town, sel_v, kv, kt, cnt, w, hits,
    meta_s, p_in, p_out, own, own_ml, part, part_ml, sib, sib_ml, comb, comb_ml, ret, ret_ml,
    att, ysend, yrecv,
    lsem, msem,
    in_s, in_r, fw_s, fw_r, sb_s, sb_r, rt_s, rt_r, y_s, y_r,
):
    bf, f32, i32 = jnp.bfloat16, jnp.float32, jnp.int32
    n = side * side
    order = offsets_in_order(side)
    reqs, heads, dim = q_hbm.shape
    blocks, tok = kv.shape[0], kv.shape[2]
    group = heads // 2
    cols = out_ref.shape[1]
    me = lax.axis_index("mem")
    y = lax.axis_index("head")
    core = me % 2
    chip = me // 2
    cx, cz = chip // side, chip % side
    sibling = me + 1 - 2 * core
    line = cz * 2 + core
    c2 = scale * LOG2E

    def chip_at(dx, dz):
        px = (cx + dx + side) % side
        pz = (cz + dz + side) % side
        return (px * side + pz) * 2 + core

    def pick(values, k):
        if isinstance(k, int):
            return values[k]
        found = i32(values[0])
        for i in range(1, n):
            found = jnp.where(k == i, i32(values[i]), found)
        return found

    def remote(src, dst, ss, rs, **device):
        return pltpu.make_async_remote_copy(
            src_ref=src, dst_ref=dst, send_sem=ss, recv_sem=rs,
            device_id=device, device_id_type=MESH,
        )

    def fw(k, stream, first=False):
        src, dst = ((tin, tout), (qin, qout))[stream]
        src = (town.at[cx], q_hbm)[stream] if first else src.at[k]
        return remote(src, dst.at[k], fw_s.at[stream, k], fw_r.at[stream, k], mem=sibling)

    def plane(k, stream):
        dx, dz = order[k]
        dst = (tin, qin)[stream]
        if dz == 0:
            src = (town.at[(cx + dx) % side], q_hbm)[stream]
            peer = chip_at(dx, 0)
        elif dx == 0:
            src = (town.at[cx], q_hbm)[stream]
            peer = chip_at(0, dz)
        else:
            src = dst.at[order.index((dx, 0))]
            peer = chip_at(0, dz)
        return remote(src, dst.at[k], in_s.at[stream, k], in_r.at[stream, k], mem=peer)

    def arrived(k, stream):
        dst = (tin, qin)[stream]
        return remote(dst.at[k], dst.at[k], in_s.at[stream, k], in_r.at[stream, k], mem=sibling)

    def meta(k, slot):
        src = (tin, tout)[slot]
        return pltpu.make_async_copy(
            src.at[k, pl.ds(line, 1)], meta_s.at[slot, k], msem.at[slot, k]
        )

    def to_sibling(k):
        return (
            remote(part.at[k], sib.at[k], sb_s.at[0, k], sb_r.at[0, k], mem=sibling),
            remote(part_ml.at[k], sib_ml.at[k], sb_s.at[1, k], sb_r.at[1, k], mem=sibling),
        )

    def to_owner(k):
        peer = chip_at(-pick([d[0] for d in order], k), -pick([d[1] for d in order], k))
        return (
            remote(comb.at[k], ret.at[k], rt_s.at[0, k], rt_r.at[0, k], mem=peer),
            remote(comb_ml.at[k], ret_ml.at[k], rt_s.at[1, k], rt_r.at[1, k], mem=peer),
        )

    loc = [
        pltpu.make_async_copy(sel_hbm, sel_v, lsem.at[0]),
        pltpu.make_async_copy(kv_hbm, kv, lsem.at[1]),
        pltpu.make_async_copy(q_hbm, qin.at[0], lsem.at[2]),
        pltpu.make_async_copy(cnt_hbm, cnt, lsem.at[3]),
    ]
    for c in loc:
        c.start()

    barrier = pltpu.get_barrier_semaphore()
    pl.semaphore_signal(barrier, inc=1, device_id={"mem": sibling}, device_id_type=MESH)
    for d in range(1, side):
        for peer in (chip_at(d, 0), chip_at(0, d)):
            pl.semaphore_signal(barrier, inc=1, device_id={"mem": peer}, device_id_type=MESH)
    for j in range(1, heads_n):
        pl.semaphore_signal(
            barrier, inc=1, device_id={"head": (y + j) % heads_n}, device_id_type=MESH
        )

    pl.semaphore_wait(barrier, 2 * (side - 1) + heads_n)

    first_sends = list(range(1, side)) + [i for i in range(n) if i and order[i][0] == 0]
    for k in first_sends:
        plane(k, 1).start()
    fw(0, 1, True).start()

    devices = 2 * n
    loc[0].wait()
    sel = sel_v[...]
    target, local = sel // blocks, sel % blocks
    dev = lax.broadcasted_iota(i32, (devices, sel.shape[1]), 0)
    lane_d = lax.broadcasted_iota(i32, (devices, 128), 1)
    table = jnp.full((devices, 128), -1, i32)
    for r in range(reqs):
        here = target[r : r + 1] == dev
        value = jnp.broadcast_to(local[r : r + 1], dev.shape)
        first = jnp.min(jnp.where(here, value, blocks), axis=1, keepdims=True)
        last = jnp.max(jnp.where(here, value, -1), axis=1, keepdims=True)
        table = jnp.where((lane_d == r) & (first < blocks), first, table)
        table = jnp.where((lane_d == reqs + r) & (last > first), last, table)
    for d in range(side):
        town[d] = table[d * 2 * side : (d + 1) * 2 * side]
    tin[0] = town[cx]
    meta(0, 0).start()

    for k in first_sends:
        plane(k, 0).start()
    fw(0, 0, True).start()

    wcopies = [
        pltpu.make_async_copy(
            w_hbm.at[:, pl.ds(pl.multiple_of(((y + j) % heads_n) * cols, 128), cols)],
            w.at[j], lsem.at[4 + j],
        )
        for j in range(heads_n)
    ]
    for c in wcopies:
        c.start()

    row = lax.broadcasted_iota(i32, (heads, tok), 0)
    lane = lax.broadcasted_iota(i32, (heads, tok), 1)
    kmask = (row // group) == (lane // (tok // 2))
    lane_h = lax.broadcasted_iota(i32, (heads, 128), 1)
    brow = lax.broadcasted_iota(i32, (blocks, 128), 0)
    zero = jnp.zeros((heads, dim), bf)

    def four(a, b, c, d):
        return jnp.concatenate(
            [jnp.concatenate([a, b], axis=1), jnp.concatenate([c, d], axis=1)], axis=0
        )

    def softmax(s0, s1, off0, off1):
        s0 = jnp.where(kmask, s0 + off0, NEG)
        s1 = jnp.where(kmask, s1 + off1, NEG)
        m = jnp.max(jnp.maximum(s0, s1), axis=1, keepdims=True)
        p0, p1 = jnp.exp2((s0 - m) * c2), jnp.exp2((s1 - m) * c2)
        return p0, p1, m, jnp.sum(p0 + p1, axis=1, keepdims=True)

    def scores(q_ref, slot, k, p_ref, ml_ref):
        ml = jnp.zeros((heads, 128), f32)
        for r in range(0, reqs, 2):
            ids = [meta_s[slot, k, 0, i] for i in (r, reqs + r, r + 1, reqs + r + 1)]
            off = [jnp.where(b < 0, NEG, 0.0) for b in ids]
            k0, k1, k2, k3 = [kt[jnp.maximum(b, 0)] for b in ids]
            lhs = four(q_ref[k, r], zero, zero, q_ref[k, r + 1])
            s = jnp.dot(lhs, four(k0, k1, k2, k3), preferred_element_type=f32)
            a0, a1, ma, la = softmax(s[:heads, :tok], s[:heads, tok:], off[0], off[1])
            b0, b1, mb, lb = softmax(s[heads:, :tok], s[heads:, tok:], off[2], off[3])
            p_ref[r // 2] = jnp.concatenate(
                [jnp.concatenate([a0, b0], axis=0).astype(bf), jnp.concatenate([a1, b1], axis=0).astype(bf)],
                axis=1,
            )
            for i, v in ((r, ma), (reqs + r, la), (r + 1, mb), (reqs + r + 1, lb)):
                ml = jnp.where(lane_h == i, v, ml)
        ml_ref[k] = ml

    def values(slot, k, p_list, emit):
        for r in range(0, reqs, 2):
            ids = [meta_s[slot, k, 0, i] for i in (r, reqs + r, r + 1, reqs + r + 1)]
            v0, v1, v2, v3 = [kv[jnp.maximum(b, 0), 1] for b in ids]
            o = jnp.dot(p_list[r // 2], four(v0, v2, v1, v3), preferred_element_type=f32)
            emit(k, r, o[:heads, :dim])
            emit(k, r + 1, o[heads:, dim:])

    def emit_own(k, r, o):
        own[k, r] = o

    def emit_part(k, r, o):
        part[k, r] = o.astype(bf)

    def load(p_ref):
        return [p_ref[i] for i in range(reqs // 2)]

    def count(k):
        for t in (tin, tout):
            hits[...] += jnp.where(t[k, pl.ds(line, 1)] == brow, 1.0, 0.0)

    def combine(k):
        a, b = own_ml[k], sib_ml[k]
        top = jnp.maximum(a, b)
        fa, fb = jnp.exp2((a - top) * c2), jnp.exp2((b - top) * c2)
        total = pltpu.roll(fa, reqs, 1) * a + pltpu.roll(fb, reqs, 1) * b
        comb_ml[k] = jnp.where(lane_h < reqs, top, total)
        for r in range(reqs):
            o = own[k, r] * fa[:, r : r + 1] + sib[k, r].astype(f32) * fb[:, r : r + 1]
            comb[k, r] = o.astype(bf)

    def send_owner(k):
        for c in to_owner(k):
            c.start()

    def turn(start, stop):
        @pl.loop(start, stop)
        def _(b):
            for i in range(4):
                kt[b * 4 + i] = kv[b * 4 + i, 0].T

    loc[1].wait()
    turn(0, blocks // 4)

    fw(0, 0).wait_recv()
    meta(0, 1).start()
    hits[...] = jnp.zeros(hits.shape, f32)
    loc[2].wait()
    meta(0, 0).wait()
    scores(qin, 0, 0, p_in, own_ml)

    for s in range(2):
        for k in range(1, side):
            arrived(k, s).wait_recv()
            for i in range(n):
                if order[i][0] == order[k][0] and order[i][1]:
                    plane(i, s).start()
            fw(k, s).start()
            if s == 0:
                meta(k, 0).start()
    @pl.loop(0, n - 1)
    def _(t):
        @pl.when((t + 2 >= side) & (t + 2 < n))
        def _():
            arrived(t + 2, 0).wait_recv()
            fw(t + 2, 0).start()
            meta(t + 2, 0).start()

        fw(t + 1, 0).wait_recv()
        meta(t + 1, 1).start()

        @pl.when(t + 1 >= side)
        def _():
            arrived(t + 1, 1).wait_recv()
            fw(t + 1, 1).start()

        fw(t, 1).wait_recv()
        meta(t, 1).wait()
        meta(t + 1, 0).wait()

        p = load(p_in)
        scores(qout, 1, t, p_out, part_ml)
        values(0, t, p, emit_own)
        p = load(p_out)
        scores(qin, 0, t + 1, p_in, own_ml)
        values(1, t, p, emit_part)
        count(t)
        for c in to_sibling(t):
            c.start()

        @pl.when(t >= 1)
        def _():
            for c in to_sibling(t - 1):
                c.wait_recv()
            combine(t - 1)

        @pl.when(t >= 2)
        def _():
            send_owner(t - 1)

    fw(n - 1, 1).wait_recv()
    meta(n - 1, 1).wait()
    p = load(p_in)
    scores(qout, 1, n - 1, p_out, part_ml)
    values(0, n - 1, p, emit_own)
    values(1, n - 1, load(p_out), emit_part)
    count(n - 1)
    for c in to_sibling(n - 1):
        c.start()
    for k in (n - 2, n - 1):
        for c in to_sibling(k):
            c.wait_recv()
        combine(k)
        send_owner(k)

    loc[3].wait()
    counts = cnt[...].astype(f32)
    decay = jnp.exp2(-lax.broadcasted_iota(i32, counts.shape, 0).astype(f32))
    here = jnp.broadcast_to(jnp.sum(hits[...], axis=1, keepdims=True), (blocks, blocks))
    eye = lax.broadcasted_iota(i32, (blocks, blocks), 0) == lax.broadcasted_iota(i32, (blocks, blocks), 1)
    heat_ref[...] = jnp.sum(decay * counts, axis=0, keepdims=True) + jnp.sum(
        jnp.where(eye, here, 0.0), axis=0, keepdims=True
    )

    ret[0] = comb[0]
    ret_ml[0] = comb_ml[0]

    def merged(start, stop):
        @pl.loop(max(start, 1), stop)
        def _(k):
            for c in to_owner(k):
                c.wait_recv()

        top = ret_ml[start]
        for k in range(start + 1, stop):
            top = jnp.maximum(top, ret_ml[k])
        den = jnp.zeros((heads, 128), f32)
        acc = [jnp.zeros((heads, dim), f32)] * reqs

        def add(k, carry):
            den, acc = carry
            f = jnp.exp2((ret_ml[k] - top) * c2)
            den += f * pltpu.roll(ret_ml[k], 128 - reqs, 1)
            return den, [acc[r] + ret[k, r].astype(f32) * f[:, r : r + 1] for r in range(reqs)]

        den, acc = lax.fori_loop(start, stop, add, (den, acc))
        return top, den, acc

    top_a, den_a, acc_a = merged(0, n - later)
    top_b, den_b, acc_b = merged(n - later, n)
    top = jnp.maximum(top_a, top_b)
    fa, fb = jnp.exp2((top_a - top) * c2), jnp.exp2((top_b - top) * c2)
    inv = 1.0 / (fa * den_a + fb * den_b)
    fa, fb = fa * inv, fb * inv
    for r in range(reqs):
        att[r] = acc_a[r] * fa[:, r : r + 1] + acc_b[r] * fb[:, r : r + 1]

    lhs = jnp.concatenate([att[:, h, :].astype(bf) for h in range(heads)], axis=1)

    for c in wcopies:
        c.wait()

    def y_copy(j):
        return remote(ysend.at[j], yrecv.at[j], y_s.at[j], y_r.at[j], head=(y + j) % heads_n)

    for j in range(1, heads_n):
        ysend[j] = jnp.dot(lhs, w[j], preferred_element_type=f32).astype(bf)
        y_copy(j).start()
    total = jnp.dot(lhs, w[0], preferred_element_type=f32).astype(bf).astype(f32)
    for j in range(1, heads_n):
        y_copy(j).wait()
        total += yrecv[j].astype(f32)
    out_ref[...] = total.astype(out_ref.dtype)

    for s in range(2):
        fw(0, s, True).wait_send()
        for k in range(1, n):
            plane(k, s).wait_send()

    @pl.loop(0, n)
    def _(k):
        for c in to_sibling(k):
            c.wait_send()

        @pl.when(k > 0)
        def _():
            for s in range(2):
                fw(k, s).wait_send()
            for c in to_owner(k):
                c.wait_send()


def hand_over(out_ref, heat_ref, out, heat):
    out[...] = out_ref[...]
    heat[...] = heat_ref[...]


def per_device(side, heads_n, queries, cache_blocks, selected, counts, output_weight):
    reqs, heads, dim = queries.shape
    blocks = cache_blocks.shape[0]
    tok = cache_blocks.shape[2] * cache_blocks.shape[3]
    kv = cache_blocks.reshape(blocks, 2, tok, dim)
    n = side * side
    cols = output_weight.shape[1] // heads_n
    bf, f32, i32 = jnp.bfloat16, jnp.float32, jnp.int32
    any_ = pl.BlockSpec(memory_space=pl.ANY)
    vmem = pl.BlockSpec(memory_space=pltpu.VMEM)
    dma = pltpu.SemaphoreType.DMA
    rows = pltpu.VMEM((n, reqs, heads, dim), bf)
    small = pltpu.VMEM((n, heads, 128), f32)
    tiles = pltpu.VMEM((n, 2 * side, 128), i32)
    out, heat = pl.pallas_call(
        functools.partial(kernel, side, heads_n, dim ** -0.5, max(2, n // 4)),
        out_shape=(
            jax.ShapeDtypeStruct((reqs, cols), bf),
            jax.ShapeDtypeStruct((1, blocks), f32),
        ),
        in_specs=[any_] * 5,
        out_specs=(vmem, vmem),
        scratch_shapes=[
            rows, rows, tiles, tiles,
            pltpu.VMEM((side, 2 * side, 128), i32),
            pltpu.VMEM(selected.shape, i32),
            pltpu.VMEM(kv.shape, bf),
            pltpu.VMEM((blocks, dim, tok), bf),
            pltpu.VMEM(counts.shape, i32),
            pltpu.VMEM((heads_n, output_weight.shape[0], cols), bf),
            pltpu.VMEM((blocks, 128), f32),
            pltpu.SMEM((2, n, 1, 128), i32),
            pltpu.VMEM((reqs // 2, 2 * heads, 2 * tok), bf),
            pltpu.VMEM((reqs // 2, 2 * heads, 2 * tok), bf),
            pltpu.VMEM((n, reqs, heads, dim), f32),
            small, rows, small, rows, small, rows, small, rows, small,
            pltpu.VMEM((reqs, heads, dim), f32),
            pltpu.VMEM((heads_n, reqs, cols), bf),
            pltpu.VMEM((heads_n, reqs, cols), bf),
            dma((4 + heads_n,)), dma((2, n)),
            dma((2, n)), dma((2, n)), dma((2, n)), dma((2, n)),
            dma((2, n)), dma((2, n)), dma((2, n)), dma((2, n)),
            dma((heads_n,)), dma((heads_n,)),
        ],
        compiler_params=pltpu.CompilerParams(collective_id=0, has_side_effects=True),
    )(queries, kv, selected, counts, output_weight)
    return pl.pallas_call(
        hand_over,
        out_shape=(jax.ShapeDtypeStruct(out.shape, bf), jax.ShapeDtypeStruct((blocks,), f32)),
        in_specs=(vmem, vmem),
        out_specs=(vmem, vmem),
    )(out, heat.reshape(blocks))


def solution(mesh):
    side = math.isqrt(mesh.shape["mem"] // 2)
    return jax.shard_map(
        functools.partial(per_device, side, mesh.shape["head"]),
        mesh=mesh,
        in_specs=(
            P("mem", "head", None),
            P("mem", None, "head", None, None),
            P("mem", None),
            P(None, "mem"),
            P("head", None),
        ),
        out_specs=(P("mem", "head"), P("mem")),
        check_vma=False,
    )
```

```python
import functools
import math

import jax
import jax.numpy as jnp
from jax import lax
from jax.experimental import pallas as pl
from jax.experimental.pallas import tpu as pltpu
from jax.sharding import PartitionSpec as P

MESH = pl.DeviceIdType.MESH
NEG = -1e30
LOG2E = 1.4426950408889634


def offsets_in_order(side):
    far = list(range(2, side - 1))
    near = [1] + ([side - 1] if side > 2 else [])
    order = [(0, 0)] + [(dx, 0) for dx in near + far] + [(0, dz) for dz in far]
    order += [(dx, dz) for dx in near for dz in near]
    order += [(dx, dz) for dx in near for dz in far]
    order += [(dx, dz) for dx in far for dz in near + far]
    return order + [(0, dz) for dz in near]


def kernel(
    side, heads_n, scale, later,
    q_hbm, kv_hbm, sel_hbm, cnt_hbm, w_hbm,
    out_ref, heat_ref,
    qin, qout, tin, tout, town, sel_v, kv, kt, cnt, w, hits,
    meta_s, p_in, p_out, own, own_ml, part, part_ml, sib, sib_ml, comb, comb_ml, ret, ret_ml,
    att, ysend, yrecv,
    lsem, msem,
    in_s, in_r, fw_s, fw_r, sb_s, sb_r, rt_s, rt_r, y_s, y_r,
):
    bf, f32, i32 = jnp.bfloat16, jnp.float32, jnp.int32
    n = side * side
    order = offsets_in_order(side)
    reqs, heads, dim = q_hbm.shape
    blocks, tok = kv.shape[0], kv.shape[2]
    group = heads // 2
    cols = out_ref.shape[1]
    me = lax.axis_index("mem")
    y = lax.axis_index("head")
    core = me % 2
    chip = me // 2
    cx, cz = chip // side, chip % side
    sibling = me + 1 - 2 * core
    line = cz * 2 + core
    c2 = scale * LOG2E

    def chip_at(dx, dz):
        px = (cx + dx + side) % side
        pz = (cz + dz + side) % side
        return (px * side + pz) * 2 + core

    def pick(values, k):
        if isinstance(k, int):
            return values[k]
        found = i32(values[0])
        for i in range(1, n):
            found = jnp.where(k == i, i32(values[i]), found)
        return found

    def remote(src, dst, ss, rs, **device):
        return pltpu.make_async_remote_copy(
            src_ref=src, dst_ref=dst, send_sem=ss, recv_sem=rs,
            device_id=device, device_id_type=MESH,
        )

    def fw(k, stream, first=False):
        src, dst = ((tin, tout), (qin, qout))[stream]
        src = (town.at[cx], q_hbm)[stream] if first else src.at[k]
        return remote(src, dst.at[k], fw_s.at[stream, k], fw_r.at[stream, k], mem=sibling)

    def plane(k, stream):
        dx, dz = order[k]
        dst = (tin, qin)[stream]
        if dz == 0:
            src = (town.at[(cx + dx) % side], q_hbm)[stream]
            peer = chip_at(dx, 0)
        elif dx == 0:
            src = (town.at[cx], q_hbm)[stream]
            peer = chip_at(0, dz)
        else:
            src = dst.at[order.index((dx, 0))]
            peer = chip_at(0, dz)
        return remote(src, dst.at[k], in_s.at[stream, k], in_r.at[stream, k], mem=peer)

    def arrived(k, stream):
        dst = (tin, qin)[stream]
        return remote(dst.at[k], dst.at[k], in_s.at[stream, k], in_r.at[stream, k], mem=sibling)

    def meta(k, slot):
        src = (tin, tout)[slot]
        return pltpu.make_async_copy(
            src.at[k, pl.ds(line, 1)], meta_s.at[slot, k], msem.at[slot, k]
        )

    def to_sibling(k):
        return (
            remote(part.at[k], sib.at[k], sb_s.at[0, k], sb_r.at[0, k], mem=sibling),
            remote(part_ml.at[k], sib_ml.at[k], sb_s.at[1, k], sb_r.at[1, k], mem=sibling),
        )

    def to_owner(k):
        peer = chip_at(-pick([d[0] for d in order], k), -pick([d[1] for d in order], k))
        return (
            remote(comb.at[k], ret.at[k], rt_s.at[0, k], rt_r.at[0, k], mem=peer),
            remote(comb_ml.at[k], ret_ml.at[k], rt_s.at[1, k], rt_r.at[1, k], mem=peer),
        )

    loc = [
        pltpu.make_async_copy(sel_hbm, sel_v, lsem.at[0]),
        pltpu.make_async_copy(kv_hbm, kv, lsem.at[1]),
        pltpu.make_async_copy(q_hbm, qin.at[0], lsem.at[2]),
        pltpu.make_async_copy(cnt_hbm, cnt, lsem.at[3]),
    ]
    barrier = pltpu.get_barrier_semaphore()
    pl.semaphore_signal(barrier, inc=1, device_id={"mem": sibling}, device_id_type=MESH)
    for d in range(1, side):
        for peer in (chip_at(d, 0), chip_at(0, d)):
            pl.semaphore_signal(barrier, inc=1, device_id={"mem": peer}, device_id_type=MESH)
    for j in range(1, heads_n):
        pl.semaphore_signal(
            barrier, inc=1, device_id={"head": (y + j) % heads_n}, device_id_type=MESH
        )

    for c in loc:
        c.start()

    pl.semaphore_wait(barrier, 2 * (side - 1) + heads_n)

    first_sends = list(range(1, side)) + [i for i in range(n) if i and order[i][0] == 0]
    for k in first_sends:
        plane(k, 1).start()
    fw(0, 1, True).start()

    devices = 2 * n
    loc[0].wait()
    sel = sel_v[...]
    target, local = sel // blocks, sel % blocks
    dev = lax.broadcasted_iota(i32, (devices, sel.shape[1]), 0)
    lane_d = lax.broadcasted_iota(i32, (devices, 128), 1)
    table = jnp.full((devices, 128), -1, i32)
    for r in range(reqs):
        here = target[r : r + 1] == dev
        value = jnp.broadcast_to(local[r : r + 1], dev.shape)
        first = jnp.min(jnp.where(here, value, blocks), axis=1, keepdims=True)
        last = jnp.max(jnp.where(here, value, -1), axis=1, keepdims=True)
        table = jnp.where((lane_d == r) & (first < blocks), first, table)
        table = jnp.where((lane_d == reqs + r) & (last > first), last, table)
    for d in range(side):
        town[d] = table[d * 2 * side : (d + 1) * 2 * side]
    tin[0] = town[cx]
    meta(0, 0).start()

    for k in first_sends:
        plane(k, 0).start()
    fw(0, 0, True).start()

    wcopies = [
        pltpu.make_async_copy(
            w_hbm.at[:, pl.ds(pl.multiple_of(((y + j) % heads_n) * cols, 128), cols)],
            w.at[j], lsem.at[4 + j],
        )
        for j in range(heads_n)
    ]
    for c in wcopies:
        c.start()

    row = lax.broadcasted_iota(i32, (heads, tok), 0)
    lane = lax.broadcasted_iota(i32, (heads, tok), 1)
    kmask = (row // group) == (lane // (tok // 2))
    lane_h = lax.broadcasted_iota(i32, (heads, 128), 1)
    brow = lax.broadcasted_iota(i32, (blocks, 128), 0)
    zero = jnp.zeros((heads, dim), bf)

    def four(a, b, c, d):
        return jnp.concatenate(
            [jnp.concatenate([a, b], axis=1), jnp.concatenate([c, d], axis=1)], axis=0
        )

    def softmax(s0, s1, off0, off1):
        s0 = jnp.where(kmask, s0 + off0, NEG)
        s1 = jnp.where(kmask, s1 + off1, NEG)
        m = jnp.max(jnp.maximum(s0, s1), axis=1, keepdims=True)
        p0, p1 = jnp.exp2((s0 - m) * c2), jnp.exp2((s1 - m) * c2)
        return p0, p1, m, jnp.sum(p0 + p1, axis=1, keepdims=True)

    def scores(q_ref, slot, k, p_ref, ml_ref):
        ml = jnp.zeros((heads, 128), f32)
        for r in range(0, reqs, 2):
            ids = [meta_s[slot, k, 0, i] for i in (r, reqs + r, r + 1, reqs + r + 1)]
            off = [jnp.where(b < 0, NEG, 0.0) for b in ids]
            k0, k1, k2, k3 = [kt[jnp.maximum(b, 0)] for b in ids]
            lhs = four(q_ref[k, r], zero, zero, q_ref[k, r + 1])
            s = jnp.dot(lhs, four(k0, k1, k2, k3), preferred_element_type=f32)
            a0, a1, ma, la = softmax(s[:heads, :tok], s[:heads, tok:], off[0], off[1])
            b0, b1, mb, lb = softmax(s[heads:, :tok], s[heads:, tok:], off[2], off[3])
            p_ref[r // 2] = jnp.concatenate(
                [jnp.concatenate([a0, b0], axis=0).astype(bf), jnp.concatenate([a1, b1], axis=0).astype(bf)],
                axis=1,
            )
            for i, v in ((r, ma), (reqs + r, la), (r + 1, mb), (reqs + r + 1, lb)):
                ml = jnp.where(lane_h == i, v, ml)
        ml_ref[k] = ml

    def values(slot, k, p_list, emit):
        for r in range(0, reqs, 2):
            ids = [meta_s[slot, k, 0, i] for i in (r, reqs + r, r + 1, reqs + r + 1)]
            v0, v1, v2, v3 = [kv[jnp.maximum(b, 0), 1] for b in ids]
            o = jnp.dot(p_list[r // 2], four(v0, v2, v1, v3), preferred_element_type=f32)
            emit(k, r, o[:heads, :dim])
            emit(k, r + 1, o[heads:, dim:])

    def emit_own(k, r, o):
        own[k, r] = o

    def emit_part(k, r, o):
        part[k, r] = o.astype(bf)

    def load(p_ref):
        return [p_ref[i] for i in range(reqs // 2)]

    def count(k):
        for t in (tin, tout):
            hits[...] += jnp.where(t[k, pl.ds(line, 1)] == brow, 1.0, 0.0)

    def combine(k):
        a, b = own_ml[k], sib_ml[k]
        top = jnp.maximum(a, b)
        fa, fb = jnp.exp2((a - top) * c2), jnp.exp2((b - top) * c2)
        total = pltpu.roll(fa, reqs, 1) * a + pltpu.roll(fb, reqs, 1) * b
        comb_ml[k] = jnp.where(lane_h < reqs, top, total)
        for r in range(reqs):
            o = own[k, r] * fa[:, r : r + 1] + sib[k, r].astype(f32) * fb[:, r : r + 1]
            comb[k, r] = o.astype(bf)

    def send_owner(k):
        for c in to_owner(k):
            c.start()

    def turn(start, stop):
        @pl.loop(start, stop)
        def _(b):
            for i in range(4):
                kt[b * 4 + i] = kv[b * 4 + i, 0].T

    loc[1].wait()
    turn(0, blocks // 4)

    fw(0, 0).wait_recv()
    meta(0, 1).start()
    hits[...] = jnp.zeros(hits.shape, f32)
    loc[2].wait()
    meta(0, 0).wait()
    scores(qin, 0, 0, p_in, own_ml)

    for s in range(2):
        for k in range(1, side):
            arrived(k, s).wait_recv()
            for i in range(n):
                if order[i][0] == order[k][0] and order[i][1]:
                    plane(i, s).start()
            fw(k, s).start()
            if s == 0:
                meta(k, 0).start()
    @pl.loop(0, n - 1)
    def _(t):
        @pl.when((t + 2 >= side) & (t + 2 < n))
        def _():
            arrived(t + 2, 0).wait_recv()
            fw(t + 2, 0).start()
            meta(t + 2, 0).start()

        fw(t + 1, 0).wait_recv()
        meta(t + 1, 1).start()

        @pl.when(t + 1 >= side)
        def _():
            arrived(t + 1, 1).wait_recv()
            fw(t + 1, 1).start()

        fw(t, 1).wait_recv()
        meta(t, 1).wait()
        meta(t + 1, 0).wait()

        @pl.when(t >= 2)
        def _():
            for c in to_sibling(t - 2):
                c.wait_recv()

        combine(jnp.where(t >= 2, t - 2, n))
        p = load(p_in)
        scores(qout, 1, t, p_out, part_ml)
        values(0, t, p, emit_own)
        p = load(p_out)
        scores(qin, 0, t + 1, p_in, own_ml)
        values(1, t, p, emit_part)
        count(t)
        for c in to_sibling(t):
            c.start()

        @pl.when(t >= 3)
        def _():
            send_owner(t - 2)

    fw(n - 1, 1).wait_recv()
    meta(n - 1, 1).wait()
    for c in to_sibling(n - 3):
        c.wait_recv()
    combine(n - 3)
    p = load(p_in)
    scores(qout, 1, n - 1, p_out, part_ml)
    values(0, n - 1, p, emit_own)
    values(1, n - 1, load(p_out), emit_part)
    count(n - 1)
    for c in to_sibling(n - 1):
        c.start()
    send_owner(n - 3)
    for k in (n - 2, n - 1):
        for c in to_sibling(k):
            c.wait_recv()
        combine(k)
        send_owner(k)

    loc[3].wait()
    counts = cnt[...].astype(f32)
    decay = jnp.exp2(-lax.broadcasted_iota(i32, counts.shape, 0).astype(f32))
    here = jnp.broadcast_to(jnp.sum(hits[...], axis=1, keepdims=True), (blocks, blocks))
    eye = lax.broadcasted_iota(i32, (blocks, blocks), 0) == lax.broadcasted_iota(i32, (blocks, blocks), 1)
    heat_ref[...] = jnp.sum(decay * counts, axis=0, keepdims=True) + jnp.sum(
        jnp.where(eye, here, 0.0), axis=0, keepdims=True
    )

    ret[0] = comb[0]
    ret_ml[0] = comb_ml[0]

    def merged(start, stop):
        @pl.loop(max(start, 1), stop)
        def _(k):
            for c in to_owner(k):
                c.wait_recv()

        top = ret_ml[start]
        for k in range(start + 1, stop):
            top = jnp.maximum(top, ret_ml[k])
        den = jnp.zeros((heads, 128), f32)
        acc = [jnp.zeros((heads, dim), f32)] * reqs

        def add(k, carry):
            den, acc = carry
            f = jnp.exp2((ret_ml[k] - top) * c2)
            den += f * pltpu.roll(ret_ml[k], 128 - reqs, 1)
            return den, [acc[r] + ret[k, r].astype(f32) * f[:, r : r + 1] for r in range(reqs)]

        den, acc = lax.fori_loop(start, stop, add, (den, acc))
        return top, den, acc

    top_a, den_a, acc_a = merged(0, n - later)
    top_b, den_b, acc_b = merged(n - later, n)
    top = jnp.maximum(top_a, top_b)
    fa, fb = jnp.exp2((top_a - top) * c2), jnp.exp2((top_b - top) * c2)
    inv = 1.0 / (fa * den_a + fb * den_b)
    fa, fb = fa * inv, fb * inv
    for r in range(reqs):
        att[r] = acc_a[r] * fa[:, r : r + 1] + acc_b[r] * fb[:, r : r + 1]

    lhs = jnp.concatenate([att[:, h, :].astype(bf) for h in range(heads)], axis=1)

    for c in wcopies:
        c.wait()

    def y_copy(j):
        return remote(ysend.at[j], yrecv.at[j], y_s.at[j], y_r.at[j], head=(y + j) % heads_n)

    for j in range(1, heads_n):
        ysend[j] = jnp.dot(lhs, w[j], preferred_element_type=f32).astype(bf)
        y_copy(j).start()
    total = jnp.dot(lhs, w[0], preferred_element_type=f32).astype(bf).astype(f32)
    for j in range(1, heads_n):
        y_copy(j).wait()
        total += yrecv[j].astype(f32)
    out_ref[...] = total.astype(out_ref.dtype)

    for s in range(2):
        fw(0, s, True).wait_send()
        for k in range(1, n):
            plane(k, s).wait_send()

    @pl.loop(0, n)
    def _(k):
        for c in to_sibling(k):
            c.wait_send()

        @pl.when(k > 0)
        def _():
            for s in range(2):
                fw(k, s).wait_send()
            for c in to_owner(k):
                c.wait_send()


def hand_over(out_ref, heat_ref, out, heat):
    out[...] = out_ref[...]
    heat[...] = heat_ref[...]


def per_device(side, heads_n, queries, cache_blocks, selected, counts, output_weight):
    reqs, heads, dim = queries.shape
    blocks = cache_blocks.shape[0]
    tok = cache_blocks.shape[2] * cache_blocks.shape[3]
    kv = cache_blocks.reshape(blocks, 2, tok, dim)
    n = side * side
    cols = output_weight.shape[1] // heads_n
    bf, f32, i32 = jnp.bfloat16, jnp.float32, jnp.int32
    any_ = pl.BlockSpec(memory_space=pl.ANY)
    vmem = pl.BlockSpec(memory_space=pltpu.VMEM)
    dma = pltpu.SemaphoreType.DMA
    rows = pltpu.VMEM((n, reqs, heads, dim), bf)
    small = pltpu.VMEM((n + 1, heads, 128), f32)
    spare = pltpu.VMEM((n + 1, reqs, heads, dim), bf)
    tiles = pltpu.VMEM((n, 2 * side, 128), i32)
    out, heat = pl.pallas_call(
        functools.partial(kernel, side, heads_n, dim ** -0.5, max(2, n // 4)),
        out_shape=(
            jax.ShapeDtypeStruct((reqs, cols), bf),
            jax.ShapeDtypeStruct((1, blocks), f32),
        ),
        in_specs=[any_] * 5,
        out_specs=(vmem, vmem),
        scratch_shapes=[
            rows, rows, tiles, tiles,
            pltpu.VMEM((side, 2 * side, 128), i32),
            pltpu.VMEM(selected.shape, i32),
            pltpu.VMEM(kv.shape, bf),
            pltpu.VMEM((blocks, dim, tok), bf),
            pltpu.VMEM(counts.shape, i32),
            pltpu.VMEM((heads_n, output_weight.shape[0], cols), bf),
            pltpu.VMEM((blocks, 128), f32),
            pltpu.SMEM((2, n, 1, 128), i32),
            pltpu.VMEM((reqs // 2, 2 * heads, 2 * tok), bf),
            pltpu.VMEM((reqs // 2, 2 * heads, 2 * tok), bf),
            pltpu.VMEM((n + 1, reqs, heads, dim), f32),
            small, rows, small, spare, small, spare, small, rows, small,
            pltpu.VMEM((reqs, heads, dim), f32),
            pltpu.VMEM((heads_n, reqs, cols), bf),
            pltpu.VMEM((heads_n, reqs, cols), bf),
            dma((4 + heads_n,)), dma((2, n)),
            dma((2, n)), dma((2, n)), dma((2, n)), dma((2, n)),
            dma((2, n)), dma((2, n)), dma((2, n)), dma((2, n)),
            dma((heads_n,)), dma((heads_n,)),
        ],
        compiler_params=pltpu.CompilerParams(collective_id=0, has_side_effects=True),
    )(queries, kv, selected, counts, output_weight)
    return pl.pallas_call(
        hand_over,
        out_shape=(jax.ShapeDtypeStruct(out.shape, bf), jax.ShapeDtypeStruct((blocks,), f32)),
        in_specs=(vmem, vmem),
        out_specs=(vmem, vmem),
    )(out, heat.reshape(blocks))


def solution(mesh):
    side = math.isqrt(mesh.shape["mem"] // 2)
    return jax.shard_map(
        functools.partial(per_device, side, mesh.shape["head"]),
        mesh=mesh,
        in_specs=(
            P("mem", "head", None),
            P("mem", None, "head", None, None),
            P("mem", None),
            P(None, "mem"),
            P("head", None),
        ),
        out_specs=(P("mem", "head"), P("mem")),
        check_vma=False,
    )
```

```python
import functools
import math

import jax
import jax.numpy as jnp
from jax import lax
from jax.experimental import pallas as pl
from jax.experimental.pallas import tpu as pltpu
from jax.sharding import PartitionSpec as P

MESH = pl.DeviceIdType.MESH
NEG = -1e30
LOG2E = 1.4426950408889634


def offsets_in_order(side):
    far = list(range(2, side - 1))
    near = [1] + ([side - 1] if side > 2 else [])
    order = [(0, 0)] + [(dx, 0) for dx in near + far] + [(0, dz) for dz in far]
    order += [(dx, dz) for dx in near for dz in near]
    order += [(dx, dz) for dx in near for dz in far]
    order += [(dx, dz) for dx in far for dz in near + far]
    return order + [(0, dz) for dz in near]


def kernel(
    side, heads_n, scale, later,
    q_hbm, kv_hbm, sel_hbm, cnt_hbm, w_hbm,
    out_ref, heat_ref,
    qin, qout, tin, tout, town, sel_v, kv, kt, cnt, w, hits,
    meta_s, p_in, p_out, own, own_ml, part, part_ml, sib, sib_ml, comb, comb_ml, ret, ret_ml,
    att, ysend, yrecv,
    lsem, msem,
    in_s, in_r, fw_s, fw_r, sb_s, sb_r, rt_s, rt_r, y_s, y_r,
):
    bf, f32, i32 = jnp.bfloat16, jnp.float32, jnp.int32
    n = side * side
    order = offsets_in_order(side)
    reqs, heads, dim = q_hbm.shape
    blocks, tok = kv.shape[0], kv.shape[2]
    group = heads // 2
    cols = out_ref.shape[1]
    me = lax.axis_index("mem")
    y = lax.axis_index("head")
    core = me % 2
    chip = me // 2
    cx, cz = chip // side, chip % side
    sibling = me + 1 - 2 * core
    line = cz * 2 + core
    c2 = scale * LOG2E

    def chip_at(dx, dz):
        px = (cx + dx + side) % side
        pz = (cz + dz + side) % side
        return (px * side + pz) * 2 + core

    def pick(values, k):
        if isinstance(k, int):
            return values[k]
        found = i32(values[0])
        for i in range(1, n):
            found = jnp.where(k == i, i32(values[i]), found)
        return found

    def remote(src, dst, ss, rs, **device):
        return pltpu.make_async_remote_copy(
            src_ref=src, dst_ref=dst, send_sem=ss, recv_sem=rs,
            device_id=device, device_id_type=MESH,
        )

    def fw(k, stream, first=False):
        src, dst = ((tin, tout), (qin, qout))[stream]
        src = (town.at[cx], q_hbm)[stream] if first else src.at[k]
        return remote(src, dst.at[k], fw_s.at[stream, k], fw_r.at[stream, k], mem=sibling)

    def plane(k, stream):
        dx, dz = order[k]
        dst = (tin, qin)[stream]
        if dz == 0:
            src = (town.at[(cx + dx) % side], q_hbm)[stream]
            peer = chip_at(dx, 0)
        elif dx == 0:
            src = (town.at[cx], q_hbm)[stream]
            peer = chip_at(0, dz)
        else:
            src = dst.at[order.index((dx, 0))]
            peer = chip_at(0, dz)
        return remote(src, dst.at[k], in_s.at[stream, k], in_r.at[stream, k], mem=peer)

    def arrived(k, stream):
        dst = (tin, qin)[stream]
        return remote(dst.at[k], dst.at[k], in_s.at[stream, k], in_r.at[stream, k], mem=sibling)

    def meta(k, slot):
        src = (tin, tout)[slot]
        return pltpu.make_async_copy(
            src.at[k, pl.ds(line, 1)], meta_s.at[slot, k], msem.at[slot, k]
        )

    def to_sibling(k):
        return (
            remote(part.at[k], sib.at[k], sb_s.at[0, k], sb_r.at[0, k], mem=sibling),
            remote(part_ml.at[k], sib_ml.at[k], sb_s.at[1, k], sb_r.at[1, k], mem=sibling),
        )

    def to_owner(k):
        peer = chip_at(-pick([d[0] for d in order], k), -pick([d[1] for d in order], k))
        return (
            remote(comb.at[k], ret.at[k], rt_s.at[0, k], rt_r.at[0, k], mem=peer),
            remote(comb_ml.at[k], ret_ml.at[k], rt_s.at[1, k], rt_r.at[1, k], mem=peer),
        )

    def straight():
        dx, dz = order[n - 1]
        peer = chip_at(-dx, -dz) + 1 - 2 * core
        return (
            remote(part.at[n - 1], ret.at[n], sb_s.at[0, n - 1], sb_r.at[0, n - 1], mem=peer),
            remote(part_ml.at[n - 1], ret_ml.at[n], sb_s.at[1, n - 1], sb_r.at[1, n - 1], mem=peer),
        )

    loc = [
        pltpu.make_async_copy(sel_hbm, sel_v, lsem.at[0]),
        pltpu.make_async_copy(kv_hbm, kv, lsem.at[1]),
        pltpu.make_async_copy(q_hbm, qin.at[0], lsem.at[2]),
        pltpu.make_async_copy(cnt_hbm, cnt, lsem.at[3]),
    ]
    for c in loc:
        c.start()

    barrier = pltpu.get_barrier_semaphore()
    pl.semaphore_signal(barrier, inc=1, device_id={"mem": sibling}, device_id_type=MESH)
    for d in range(1, side):
        for peer in (chip_at(d, 0), chip_at(0, d)):
            pl.semaphore_signal(barrier, inc=1, device_id={"mem": peer}, device_id_type=MESH)
    for j in range(1, heads_n):
        pl.semaphore_signal(
            barrier, inc=1, device_id={"head": (y + j) % heads_n}, device_id_type=MESH
        )

    pl.semaphore_wait(barrier, 2 * (side - 1) + heads_n)

    first_sends = list(range(1, side)) + [i for i in range(n) if i and order[i][0] == 0]
    for k in first_sends:
        plane(k, 1).start()
    fw(0, 1, True).start()

    devices = 2 * n
    loc[0].wait()
    sel = sel_v[...]
    target, local = sel // blocks, sel % blocks
    dev = lax.broadcasted_iota(i32, (devices, sel.shape[1]), 0)
    lane_d = lax.broadcasted_iota(i32, (devices, 128), 1)
    table = jnp.full((devices, 128), -1, i32)
    for r in range(reqs):
        here = target[r : r + 1] == dev
        value = jnp.broadcast_to(local[r : r + 1], dev.shape)
        first = jnp.min(jnp.where(here, value, blocks), axis=1, keepdims=True)
        last = jnp.max(jnp.where(here, value, -1), axis=1, keepdims=True)
        table = jnp.where((lane_d == r) & (first < blocks), first, table)
        table = jnp.where((lane_d == reqs + r) & (last > first), last, table)
    for d in range(side):
        town[d] = table[d * 2 * side : (d + 1) * 2 * side]
    tin[0] = town[cx]
    meta(0, 0).start()

    for k in first_sends:
        plane(k, 0).start()
    fw(0, 0, True).start()

    wcopies = [
        pltpu.make_async_copy(
            w_hbm.at[:, pl.ds(pl.multiple_of(((y + j) % heads_n) * cols, 128), cols)],
            w.at[j], lsem.at[4 + j],
        )
        for j in range(heads_n)
    ]
    for c in wcopies:
        c.start()

    row = lax.broadcasted_iota(i32, (heads, tok), 0)
    lane = lax.broadcasted_iota(i32, (heads, tok), 1)
    kmask = (row // group) == (lane // (tok // 2))
    lane_h = lax.broadcasted_iota(i32, (heads, 128), 1)
    brow = lax.broadcasted_iota(i32, (blocks, 128), 0)
    zero = jnp.zeros((heads, dim), bf)

    def four(a, b, c, d):
        return jnp.concatenate(
            [jnp.concatenate([a, b], axis=1), jnp.concatenate([c, d], axis=1)], axis=0
        )

    def softmax(s0, s1, off0, off1):
        s0 = jnp.where(kmask, s0 + off0, NEG)
        s1 = jnp.where(kmask, s1 + off1, NEG)
        m = jnp.max(jnp.maximum(s0, s1), axis=1, keepdims=True)
        p0, p1 = jnp.exp2((s0 - m) * c2), jnp.exp2((s1 - m) * c2)
        return p0, p1, m, jnp.sum(p0 + p1, axis=1, keepdims=True)

    def scores(q_ref, slot, k, p_ref, ml_ref):
        ml = jnp.zeros((heads, 128), f32)
        for r in range(0, reqs, 2):
            ids = [meta_s[slot, k, 0, i] for i in (r, reqs + r, r + 1, reqs + r + 1)]
            off = [jnp.where(b < 0, NEG, 0.0) for b in ids]
            k0, k1, k2, k3 = [kt[jnp.maximum(b, 0)] for b in ids]
            lhs = four(q_ref[k, r], zero, zero, q_ref[k, r + 1])
            s = jnp.dot(lhs, four(k0, k1, k2, k3), preferred_element_type=f32)
            a0, a1, ma, la = softmax(s[:heads, :tok], s[:heads, tok:], off[0], off[1])
            b0, b1, mb, lb = softmax(s[heads:, :tok], s[heads:, tok:], off[2], off[3])
            p_ref[r // 2] = jnp.concatenate(
                [jnp.concatenate([a0, b0], axis=0).astype(bf), jnp.concatenate([a1, b1], axis=0).astype(bf)],
                axis=1,
            )
            for i, v in ((r, ma), (reqs + r, la), (r + 1, mb), (reqs + r + 1, lb)):
                ml = jnp.where(lane_h == i, v, ml)
        ml_ref[k] = ml

    def values(slot, k, p_list, emit):
        for r in range(0, reqs, 2):
            ids = [meta_s[slot, k, 0, i] for i in (r, reqs + r, r + 1, reqs + r + 1)]
            v0, v1, v2, v3 = [kv[jnp.maximum(b, 0), 1] for b in ids]
            o = jnp.dot(p_list[r // 2], four(v0, v2, v1, v3), preferred_element_type=f32)
            emit(k, r, o[:heads, :dim])
            emit(k, r + 1, o[heads:, dim:])

    def emit_own(k, r, o):
        own[k, r] = o

    def emit_part(k, r, o):
        part[k, r] = o.astype(bf)

    def emit_last(k, r, o):
        comb[k, r] = o.astype(bf)

    def load(p_ref):
        return [p_ref[i] for i in range(reqs // 2)]

    def count(k):
        for t in (tin, tout):
            hits[...] += jnp.where(t[k, pl.ds(line, 1)] == brow, 1.0, 0.0)

    def combine(k):
        a, b = own_ml[k], sib_ml[k]
        top = jnp.maximum(a, b)
        fa, fb = jnp.exp2((a - top) * c2), jnp.exp2((b - top) * c2)
        total = pltpu.roll(fa, reqs, 1) * a + pltpu.roll(fb, reqs, 1) * b
        comb_ml[k] = jnp.where(lane_h < reqs, top, total)
        for r in range(reqs):
            o = own[k, r] * fa[:, r : r + 1] + sib[k, r].astype(f32) * fb[:, r : r + 1]
            comb[k, r] = o.astype(bf)

    def send_owner(k):
        for c in to_owner(k):
            c.start()

    def turn(start, stop):
        @pl.loop(start, stop)
        def _(b):
            for i in range(4):
                kt[b * 4 + i] = kv[b * 4 + i, 0].T

    loc[1].wait()
    turn(0, blocks // 4)

    fw(0, 0).wait_recv()
    meta(0, 1).start()
    hits[...] = jnp.zeros(hits.shape, f32)
    loc[2].wait()
    meta(0, 0).wait()
    scores(qin, 0, 0, p_in, own_ml)

    for s in range(2):
        for k in range(1, side):
            arrived(k, s).wait_recv()
            for i in range(n):
                if order[i][0] == order[k][0] and order[i][1]:
                    plane(i, s).start()
            fw(k, s).start()
            if s == 0:
                meta(k, 0).start()
    @pl.loop(0, n - 1)
    def _(t):
        @pl.when((t + 2 >= side) & (t + 2 < n))
        def _():
            arrived(t + 2, 0).wait_recv()
            fw(t + 2, 0).start()
            meta(t + 2, 0).start()

        fw(t + 1, 0).wait_recv()
        meta(t + 1, 1).start()

        @pl.when(t + 1 >= side)
        def _():
            arrived(t + 1, 1).wait_recv()
            fw(t + 1, 1).start()

        fw(t, 1).wait_recv()
        meta(t, 1).wait()
        meta(t + 1, 0).wait()

        @pl.when(t >= 2)
        def _():
            for c in to_sibling(t - 2):
                c.wait_recv()

        combine(jnp.where(t >= 2, t - 2, n))
        p = load(p_in)
        scores(qout, 1, t, p_out, part_ml)
        values(0, t, p, emit_own)
        p = load(p_out)
        scores(qin, 0, t + 1, p_in, own_ml)
        values(1, t, p, emit_part)
        count(t)
        for c in to_sibling(t):
            c.start()

        @pl.when(t >= 3)
        def _():
            send_owner(t - 2)

    fw(n - 1, 1).wait_recv()
    meta(n - 1, 1).wait()
    for c in to_sibling(n - 3):
        c.wait_recv()
    combine(n - 3)
    p = load(p_in)
    scores(qout, 1, n - 1, p_out, part_ml)
    values(0, n - 1, p, emit_last)
    values(1, n - 1, load(p_out), emit_part)
    comb_ml[n - 1] = own_ml[n - 1]
    count(n - 1)
    for c in straight():
        c.start()
    send_owner(n - 1)
    send_owner(n - 3)
    for c in to_sibling(n - 2):
        c.wait_recv()
    combine(n - 2)
    send_owner(n - 2)

    loc[3].wait()
    counts = cnt[...].astype(f32)
    decay = jnp.exp2(-lax.broadcasted_iota(i32, counts.shape, 0).astype(f32))
    here = jnp.broadcast_to(jnp.sum(hits[...], axis=1, keepdims=True), (blocks, blocks))
    eye = lax.broadcasted_iota(i32, (blocks, blocks), 0) == lax.broadcasted_iota(i32, (blocks, blocks), 1)
    heat_ref[...] = jnp.sum(decay * counts, axis=0, keepdims=True) + jnp.sum(
        jnp.where(eye, here, 0.0), axis=0, keepdims=True
    )

    ret[0] = comb[0]
    ret_ml[0] = comb_ml[0]

    def merged(start, stop):
        @pl.loop(max(start, 1), min(stop, n))
        def _(k):
            for c in to_owner(k):
                c.wait_recv()

        if stop > n:
            for c in straight():
                c.wait_recv()

        top = ret_ml[start]
        for k in range(start + 1, stop):
            top = jnp.maximum(top, ret_ml[k])
        den = jnp.zeros((heads, 128), f32)
        acc = [jnp.zeros((heads, dim), f32)] * reqs

        def add(k, carry):
            den, acc = carry
            f = jnp.exp2((ret_ml[k] - top) * c2)
            den += f * pltpu.roll(ret_ml[k], 128 - reqs, 1)
            return den, [acc[r] + ret[k, r].astype(f32) * f[:, r : r + 1] for r in range(reqs)]

        den, acc = lax.fori_loop(start, stop, add, (den, acc))
        return top, den, acc

    top_a, den_a, acc_a = merged(0, n - later)
    top_b, den_b, acc_b = merged(n - later, n + 1)
    top = jnp.maximum(top_a, top_b)
    fa, fb = jnp.exp2((top_a - top) * c2), jnp.exp2((top_b - top) * c2)
    inv = 1.0 / (fa * den_a + fb * den_b)
    fa, fb = fa * inv, fb * inv
    for r in range(reqs):
        att[r] = acc_a[r] * fa[:, r : r + 1] + acc_b[r] * fb[:, r : r + 1]

    lhs = jnp.concatenate([att[:, h, :].astype(bf) for h in range(heads)], axis=1)

    for c in wcopies:
        c.wait()

    def y_copy(j):
        return remote(ysend.at[j], yrecv.at[j], y_s.at[j], y_r.at[j], head=(y + j) % heads_n)

    for j in sorted(range(1, heads_n), key=lambda j: -min(j, heads_n - j)):
        ysend[j] = jnp.dot(lhs, w[j], preferred_element_type=f32).astype(bf)
        y_copy(j).start()
    total = jnp.dot(lhs, w[0], preferred_element_type=f32).astype(bf).astype(f32)
    for j in range(1, heads_n):
        y_copy(j).wait()
        total += yrecv[j].astype(f32)
    out_ref[...] = total.astype(out_ref.dtype)

    for s in range(2):
        fw(0, s, True).wait_send()
        for k in range(1, n):
            plane(k, s).wait_send()

    for c in straight():
        c.wait_send()

    @pl.loop(1, n)
    def _(k):
        for c in to_sibling(k - 1):
            c.wait_send()
        for s in range(2):
            fw(k, s).wait_send()
        for c in to_owner(k):
            c.wait_send()


def hand_over(out_ref, heat_ref, out, heat):
    out[...] = out_ref[...]
    heat[...] = heat_ref[...]


def per_device(side, heads_n, queries, cache_blocks, selected, counts, output_weight):
    reqs, heads, dim = queries.shape
    blocks = cache_blocks.shape[0]
    tok = cache_blocks.shape[2] * cache_blocks.shape[3]
    kv = cache_blocks.reshape(blocks, 2, tok, dim)
    n = side * side
    cols = output_weight.shape[1] // heads_n
    bf, f32, i32 = jnp.bfloat16, jnp.float32, jnp.int32
    any_ = pl.BlockSpec(memory_space=pl.ANY)
    vmem = pl.BlockSpec(memory_space=pltpu.VMEM)
    dma = pltpu.SemaphoreType.DMA
    rows = pltpu.VMEM((n, reqs, heads, dim), bf)
    small = pltpu.VMEM((n + 1, heads, 128), f32)
    spare = pltpu.VMEM((n + 1, reqs, heads, dim), bf)
    tiles = pltpu.VMEM((n, 2 * side, 128), i32)
    out, heat = pl.pallas_call(
        functools.partial(kernel, side, heads_n, dim ** -0.5, max(1, n // 5)),
        out_shape=(
            jax.ShapeDtypeStruct((reqs, cols), bf),
            jax.ShapeDtypeStruct((1, blocks), f32),
        ),
        in_specs=[any_] * 5,
        out_specs=(vmem, vmem),
        scratch_shapes=[
            rows, rows, tiles, tiles,
            pltpu.VMEM((side, 2 * side, 128), i32),
            pltpu.VMEM(selected.shape, i32),
            pltpu.VMEM(kv.shape, bf),
            pltpu.VMEM((blocks, dim, tok), bf),
            pltpu.VMEM(counts.shape, i32),
            pltpu.VMEM((heads_n, output_weight.shape[0], cols), bf),
            pltpu.VMEM((blocks, 128), f32),
            pltpu.SMEM((2, n, 1, 128), i32),
            pltpu.VMEM((reqs // 2, 2 * heads, 2 * tok), bf),
            pltpu.VMEM((reqs // 2, 2 * heads, 2 * tok), bf),
            pltpu.VMEM((n + 1, reqs, heads, dim), f32),
            small, rows, small, spare, small, spare, small, spare, small,
            pltpu.VMEM((reqs, heads, dim), f32),
            pltpu.VMEM((heads_n, reqs, cols), bf),
            pltpu.VMEM((heads_n, reqs, cols), bf),
            dma((4 + heads_n,)), dma((2, n)),
            dma((2, n)), dma((2, n)), dma((2, n)), dma((2, n)),
            dma((2, n)), dma((2, n)), dma((2, n)), dma((2, n)),
            dma((heads_n,)), dma((heads_n,)),
        ],
        compiler_params=pltpu.CompilerParams(collective_id=0, has_side_effects=True),
    )(queries, kv, selected, counts, output_weight)
    return pl.pallas_call(
        hand_over,
        out_shape=(jax.ShapeDtypeStruct(out.shape, bf), jax.ShapeDtypeStruct((blocks,), f32)),
        in_specs=(vmem, vmem),
        out_specs=(vmem, vmem),
    )(out, heat.reshape(blocks))


def solution(mesh):
    side = math.isqrt(mesh.shape["mem"] // 2)
    return jax.shard_map(
        functools.partial(per_device, side, mesh.shape["head"]),
        mesh=mesh,
        in_specs=(
            P("mem", "head", None),
            P("mem", None, "head", None, None),
            P("mem", None),
            P(None, "mem"),
            P("head", None),
        ),
        out_specs=(P("mem", "head"), P("mem")),
        check_vma=False,
    )
```
